32 devices in a mesh: grp: 2 (over y), feat: 4 (over z), rows: 4 (over x, core).
Axes of the slice: x: 2, y: 2, z: 4, core: 2. Of those that a mesh axis runs over, the one named last changes fastest.
Arguments:
- tile_values: bfloat16 [3072, 128, 128], P(('grp', 'feat', 'rows')), parts along dimension 0, may hold values from -6 to 6
- tile_row: int32 [3072], P(('grp', 'feat', 'rows')), parts along dimension 0, may hold values from 0 to 7
- tile_block: int32 [3072], P(('grp', 'feat', 'rows')), parts along dimension 0, may hold values from 0 to 47
- tile_count: int32 [3072], P(('grp', 'feat', 'rows')), parts along dimension 0, may hold values from 1 to 16384
- tile_owner: int32 [3072, 1], P(('grp', 'feat', 'rows')), parts along dimension 0, may hold values from 0 to 3, as said below
- cut_index: int32 [31, 49152], P(None, ('grp', 'feat')), parts along dimension 1, may hold values from 0 to 309, as said below
- gradients: bfloat16 [8, 32768], P(None, ('grp', 'feat', 'rows')), parts along dimension 1, may hold values from -6 to 6
Outputs:
- histogram: float32 [8, 32, 49152], P(None, None, ('grp', 'feat', 'rows')), parts along dimension 2
The draws below stay inside these ranges and needn't reach their ends.
There are 2 independent parts, one for each index of `grp`. The reference program is written for one: setup_inputs(seed, part) draws one part's arguments, and reference() takes and returns one part's arrays. A program takes and returns all parts, laid end to end along the dimension named above; each array names one. Nothing has to cross between parts.
Inputs may be any that keep to these rules, and one draw needn't show every extreme that they name: `tile_owner`: at most 48 of the tiles of one device have the same feature group, and in every draw some feature group receives exactly 48 tiles from every device. `cut_index`: each feature's cut indices rise strictly along the first dimension.
All inputs are finite; a program needn't handle non-finite values.
Results may differ from the reference program's by a relative error of at most 0.007.
Values may be sent and summed in bfloat16 or wider, within the bound.
No kernel may reach another device: no remote copies, remote signals or barrier semaphores. Data moves between devices by JAX's collectives and lax.ppermute only.
A program may use at most 64 MiB of HBM per device.

```python
import math
import jax
import jax.numpy as jnp
from jax import lax

K = 8
BINS = 32
TILE = 128
FB_DEV = 48
TILE_DEV = 96
RB_DEV = 8
OWNERS = 4
ROW_GROUPS = 4
CAP = 48
TILES = 1536
ROWS_DEV = 1024
ROWS = 16384
FEATURES = 24576


def draw_tile_owner(key, part):
    key_top, key_rows = jax.random.split(jax.random.fold_in(key, 17))
    busiest = jax.random.randint(key_top, (), 0, OWNERS)
    keys = jax.random.split(key_rows, OWNERS * ROW_GROUPS)

    def one_device(sub):
        key_pool, key_order = jax.random.split(sub)
        others = jnp.arange((OWNERS - 1) * CAP, dtype=jnp.int32) // CAP
        others = others + (others >= busiest).astype(jnp.int32)
        chosen = jax.random.permutation(key_pool, others)[:TILE_DEV - CAP]
        whole = jnp.concatenate([jnp.zeros((CAP,), jnp.int32) + busiest, chosen])
        return jax.random.permutation(key_order, whole)
    return jax.vmap(one_device)(keys).reshape(TILES, 1).astype(jnp.int32)


def draw_tile_count(key, part):
    key_vals, key_spot = jax.random.split(jax.random.fold_in(key, 23))
    counts = jax.random.randint(key_vals, (TILES,), 1, TILE * TILE + 1)
    spot = jax.random.randint(key_spot, (), 0, TILES)
    place = jnp.arange(TILES, dtype=jnp.int32)
    counts = jnp.where(place == spot, TILE * TILE, counts)
    counts = jnp.where(place == (spot + 1) % TILES, 1, counts)
    return counts.astype(jnp.int32)


def draw_cut_index(key, part):
    offsets = jax.random.randint(jax.random.fold_in(key, 31), (BINS - 1, FEATURES), 0, 10)
    steps_up = 10 * jnp.arange(BINS - 1, dtype=jnp.int32)[:, None]
    return (steps_up + offsets).astype(jnp.int32)


def with_ends(values, own_key, smallest, top_value):
    dims = values.shape
    index_at = [jax.random.randint(jax.random.fold_in(own_key, axis), (), 0, dims[axis]) for axis in range(len(dims))]
    values = values.at[tuple(index_at)].set(smallest)
    longest = dims.index(max(dims))
    index_at[longest] = (index_at[longest] + 1) % dims[longest]
    return values.at[tuple(index_at)].set(top_value)


def block_levels(own_key, extent, pieces, low, top_value):
    gain, own = 1.0, jax.random.fold_in(own_key, 6)
    for position, parts in pieces:
        draws = jnp.exp(jax.random.uniform(jax.random.fold_in(own, position), (parts,), jnp.float32, low / len(pieces), top_value / len(pieces)))
        gain = gain * jnp.repeat(draws, extent[position] // parts).reshape([-1 if axis == position else 1 for axis in range(len(extent))])
    return gain


def noise(key, shape, scale, reach, pieces=(), held_as=jnp.bfloat16):
    values = scale * jax.random.normal(key, shape, jnp.float32)
    if pieces:
        values = values * block_levels(key, shape, pieces, -0.22, 0.18)
    return jnp.clip(values, -reach, reach).astype(held_as)


def setup_inputs(seed: int = 0, part: int = 0) -> dict:
    seeds = jax.random.split(jax.random.key(seed), 8)
    part_splits = jax.random.split(jax.random.fold_in(seeds[7], part), 8)
    return {
        "tile_values": noise(part_splits[0], (TILES, TILE, TILE), 1.0, 6.0, ((0, 16),)),
        "tile_row": with_ends(jax.random.randint(part_splits[1], (TILES,), 0, RB_DEV), jax.random.fold_in(part_splits[1], 1), 0, RB_DEV - 1).astype(jnp.int32),
        "tile_block": with_ends(jax.random.randint(part_splits[2], (TILES,), 0, FB_DEV), jax.random.fold_in(part_splits[2], 1), 0, FB_DEV - 1).astype(jnp.int32),
        "tile_count": draw_tile_count(jax.random.fold_in(jax.random.fold_in(seeds[7], part), 71), part),
        "tile_owner": draw_tile_owner(jax.random.fold_in(jax.random.fold_in(seeds[7], part), 71), part),
        "cut_index": draw_cut_index(jax.random.fold_in(jax.random.fold_in(seeds[7], part), 71), part),
        "gradients": noise(part_splits[6], (K, ROWS), 1.0, 6.0, ((1, 16),)),
    }


def reference(tile_values, tile_row, tile_block, tile_count, tile_owner, cut_index, gradients):
    cuts = (cut_index.astype(jnp.float32) + (0.5 - 5.0 * (BINS - 1))) / 64.0
    total_feat = FB_DEV * TILE * OWNERS
    per_group = OWNERS * TILE_DEV
    width = math.gcd(per_group, 256)
    flat_pos = jnp.arange(TILE, dtype=jnp.int32)[:, None] * TILE + jnp.arange(TILE, dtype=jnp.int32)[None, :]
    column = jnp.arange(TILE, dtype=jnp.int32)
    result = jnp.zeros((K, BINS, total_feat), jnp.float32)
    for group in range(ROW_GROUPS):
        def pick(a):
            shaped = a.reshape((OWNERS, ROW_GROUPS, TILE_DEV) + a.shape[1:])[:, group]
            return shaped.reshape((per_group,) + a.shape[1:])
        values = pick(tile_values)
        rows_in = pick(tile_row)
        blocks = pick(tile_block)
        counts = pick(tile_count)
        owners = pick(tile_owner)[:, 0]
        device = jnp.broadcast_to((jnp.arange(OWNERS, dtype=jnp.int32) * ROW_GROUPS + group)[:, None], (OWNERS, TILE_DEV)).reshape(per_group)
        base = device * ROWS_DEV + rows_in * TILE
        fglob = owners * FB_DEV + blocks
        turns = per_group // width

        def step(hist, x):
            vals, bases, fgs, cnts = x
            vfloat = vals.astype(jnp.float32)
            colf = (fgs[:, None] * TILE + column[None, :]).astype(jnp.int32)
            level = jnp.zeros(vals.shape, jnp.int32)
            for c in range(BINS - 1):
                level = level + (vfloat > cuts[c][colf][:, None, :]).astype(jnp.int32)
            live = flat_pos[None] < cnts[:, None, None]
            rowidx = (bases[:, None] + column[None, :]).astype(jnp.int32)
            grads = gradients[:, rowidx].astype(jnp.float32)
            data = jnp.transpose(grads, (1, 2, 0))[:, :, None, :]
            data = jnp.where(live[..., None], jnp.broadcast_to(data, (width, TILE, TILE, K)), 0.0)
            seg = (colf[:, None, :] * BINS + level).astype(jnp.int32)
            hist = hist + jax.ops.segment_sum(data.reshape(-1, K), seg.reshape(-1), num_segments=total_feat * BINS)
            return hist, None

        xs = (values.reshape(turns, width, TILE, TILE), base.reshape(turns, width), fglob.reshape(turns, width), counts.reshape(turns, width))
        hist, _ = lax.scan(step, jnp.zeros((total_feat * BINS, K), jnp.float32), xs)
        partial_value = jnp.transpose(hist.reshape(total_feat, BINS, K), (2, 1, 0)).astype(jnp.bfloat16)
        partial_value = lax.optimization_barrier(partial_value)
        result = result + partial_value.astype(jnp.float32)
    return result
```

```python
import functools

import jax
import jax.numpy as jnp
from jax import lax
from jax.experimental import pallas as pl
from jax.experimental.pallas import tpu as pltpu
from jax.sharding import PartitionSpec as P

ROWS_G = 16
VMEM = pltpu.VMEM
SMEM = pltpu.SMEM
HBM = pl.ANY
BF16 = jnp.bfloat16
FIELDS = 6


def params(mib):
    return pltpu.CompilerParams(vmem_limit_bytes=mib << 20)


def spec(space):
    return pl.BlockSpec(memory_space=space)


def granules(count, tile):
    per = ROWS_G * tile
    return (count + (per - 1)) // per


def pack_kernel(
    sizes, tile, owner_ref, count_ref, values_ref, head_ref, *rest
):
    outs, (scratch, cursor, sem, value_sem) = rest[: len(sizes)], rest[len(sizes) :]
    owners, tiles = scratch.shape[0], values_ref.shape[0]
    per_tile = tile // ROWS_G
    for o in range(owners):
        cursor[o] = 0

    def place(t, carry):
        o = owner_ref[t]
        at = cursor[o]
        cursor[o] = at + granules(count_ref[t], tile)
        scratch[o, pl.ds(at, per_tile)] = values_ref[t].reshape(per_tile, ROWS_G, tile)
        return carry

    lax.fori_loop(0, tiles, place, 0)
    head = head_ref.shape[0]
    copies = []
    start = 0
    for number, (out, size) in enumerate(zip(outs, sizes)):
        copies.append(
            pltpu.make_async_copy(
                scratch.at[:, pl.ds(start, size)],
                out.at[:, pl.ds(head if number == 0 else 0, size)],
                sem.at[number],
            )
        )
        start += size
    for o in range(owners):
        copies.append(
            pltpu.make_async_copy(
                head_ref, outs[0].at[o, pl.ds(0, head)], value_sem.at[o]
            )
        )
    for copy in copies:
        copy.start()
    for copy in copies:
        copy.wait()


def pack(owner, count, values, head, sizes, room):
    tiles, tile = values.shape[0], values.shape[1]
    owners = room[0]
    extra = [head.shape[0]] + [0] * (len(sizes) - 1)
    return pl.pallas_call(
        functools.partial(pack_kernel, sizes, tile),
        out_shape=[
            jax.ShapeDtypeStruct((owners, size + more, ROWS_G, tile), BF16)
            for size, more in zip(sizes, extra)
        ],
        in_specs=[spec(SMEM), spec(SMEM), spec(VMEM), spec(VMEM)],
        out_specs=[spec(HBM)] * len(sizes),
        scratch_shapes=[
            VMEM((owners, room[1], ROWS_G, tile), BF16),
            SMEM((owners,), jnp.int32),
            pltpu.SemaphoreType.DMA((len(sizes),)),
            pltpu.SemaphoreType.DMA((owners,)),
        ],
        compiler_params=params(24),
        cost_estimate=pl.CostEstimate(flops=0, bytes_accessed=8 << 20, transcendentals=0),
    )(owner, count, values, head)


def list_kernel(tile, row_blocks, window_ref, meta_ref, list_ref, total_ref, cursor):
    me, low, high = window_ref[0], window_ref[1], window_ref[2]
    senders, tiles = meta_ref.shape[0], meta_ref.shape[2]
    per = ROWS_G * tile
    length = high - low
    margin = tile // ROWS_G
    total_ref[1] = 0

    def sender(s, found):
        def clear(o, carry):
            cursor[o] = 0
            return carry

        lax.fori_loop(0, senders, clear, 0)

        def step(t, found):
            o = meta_ref[s, 0, t]
            count = meta_ref[s, 1, t] * tile + meta_ref[s, 2, t]
            at = cursor[o]
            end = at + granules(count, tile)
            cursor[o] = end
            total_ref[1] = jnp.maximum(total_ref[1], end)
            hit = (o == me) & (at < high) & (end > low)

            @pl.when(hit)
            def _():
                list_ref[0, found] = margin + s * length + at - low
                list_ref[1, found] = meta_ref[s, 3, t]
                list_ref[2, found] = s * row_blocks + meta_ref[s, 4, t]
                list_ref[3, found] = jnp.minimum(count, (high - at) * per)
                list_ref[4, found] = jnp.maximum(low - at, 0) * ROWS_G

            return found + hit.astype(jnp.int32)

        return lax.fori_loop(0, tiles, step, found)

    found = lax.fori_loop(0, senders, sender, 0)
    total_ref[0] = found
    list_ref[0, found] = margin
    list_ref[1, found] = 0
    list_ref[2, found] = 0
    list_ref[3, found] = 0
    list_ref[4, found] = 0


def list_tiles(window, meta, tile, row_blocks, room):
    return pl.pallas_call(
        functools.partial(list_kernel, tile, row_blocks),
        out_shape=[
            jax.ShapeDtypeStruct((FIELDS, room), jnp.int32),
            jax.ShapeDtypeStruct((2,), jnp.int32),
        ],
        in_specs=[spec(SMEM), spec(SMEM)],
        out_specs=[spec(SMEM), spec(SMEM)],
        scratch_shapes=[SMEM((meta.shape[0],), jnp.int32)],
        compiler_params=params(1),
        cost_estimate=pl.CostEstimate(flops=0, bytes_accessed=1 << 20, transcendentals=0),
    )(window, meta)


def hist_kernel(
    first, skip, list_ref, total_ref, got_ref, grads_ref, cuts_ref, *rest
):
    if first:
        hist_ref, got, sem = rest
    else:
        before_ref, hist_ref, got, sem = rest
    senders, length = got_ref.shape[0], got_ref.shape[1] - skip
    tile = got_ref.shape[3]
    per_tile = tile // ROWS_G
    levels = cuts_ref.shape[1]
    k_out = hist_ref.shape[2]
    copies = [
        pltpu.make_async_copy(
            got_ref.at[s, pl.ds(skip, length)],
            got.at[pl.ds(per_tile + s * length, length)],
            sem.at[s],
        )
        for s in range(senders)
    ]
    if not first:
        copies.append(pltpu.make_async_copy(before_ref, hist_ref, sem.at[senders]))
    for copy in copies:
        copy.start()
    if first:

        def clear(b, carry):
            hist_ref[b] = jnp.zeros(hist_ref.shape[1:], jnp.float32)
            return carry

        lax.fori_loop(0, hist_ref.shape[0], clear, 0)
    for copy in copies:
        copy.wait()
    row = lax.broadcasted_iota(jnp.int32, (tile, tile), 0).astype(jnp.float32).astype(BF16)
    lane = lax.broadcasted_iota(jnp.int32, (tile, tile), 1).astype(jnp.float32).astype(BF16)

    def as_bf16(x):
        return x.astype(jnp.float32).astype(BF16)

    def load(p):
        block = list_ref[1, p]
        count = list_ref[3, p]
        values = got[pl.ds(list_ref[0, p], per_tile)].reshape(tile, tile)
        whole = as_bf16(count // tile)
        part = as_bf16(count % tile)
        low = as_bf16(list_ref[4, p])
        live = ((row < whole) | ((row == whole) & (lane < part))) & (row >= low)
        values = jnp.where(live, values, jnp.full_like(values, -1000.0))
        return block, values

    one, zero = jnp.ones((tile, tile), BF16), jnp.zeros((tile, tile), BF16)

    def pair(i, carry):
        pa = 2 * i
        pb = 2 * i + 1
        block_a, va = load(pa)
        block_b, vb = load(pb)
        left = jnp.concatenate(
            [grads_ref[0, list_ref[2, pa]], grads_ref[1, list_ref[2, pb]]], axis=1
        )
        for c in range(0, levels, 2):
            columns = []
            for d in (c, c + 1):
                cut_a = jnp.tile(cuts_ref[block_a, d], (per_tile, 1))
                cut_b = jnp.tile(cuts_ref[block_b, d], (per_tile, 1))
                columns.append(
                    jnp.concatenate(
                        [jnp.where(va > cut_a, one, zero), jnp.where(vb > cut_b, one, zero)],
                        axis=0,
                    )
                )
            sums = jnp.dot(
                left, jnp.concatenate(columns, axis=1), preferred_element_type=jnp.float32
            )
            hist_ref[block_a, c] += sums[:k_out, :tile]
            hist_ref[block_a, c + 1] += sums[:k_out, tile:]
            hist_ref[block_b, c] += sums[k_out:, :tile]
            hist_ref[block_b, c + 1] += sums[k_out:, tile:]
        return carry

    lax.fori_loop(0, (total_ref[0] + 1) // 2, pair, 0)


def add_tiles(hist, listed, total, got, grads, cuts, skip, k_out):
    first = hist is None
    senders, length, tile = got.shape[0], got.shape[1] - skip, got.shape[3]
    blocks, levels = cuts.shape[0], cuts.shape[1]
    args = [listed, total, got, grads, cuts] + ([] if first else [hist])
    return pl.pallas_call(
        functools.partial(hist_kernel, first, skip),
        out_shape=jax.ShapeDtypeStruct((blocks, levels, k_out, tile), jnp.float32),
        in_specs=[spec(SMEM), spec(SMEM), spec(HBM), spec(VMEM), spec(VMEM)]
        + ([] if first else [spec(HBM)]),
        out_specs=spec(VMEM),
        scratch_shapes=[
            VMEM((senders * length + 2 * (tile // ROWS_G), ROWS_G, tile), BF16),
            pltpu.SemaphoreType.DMA((senders + 1,)),
        ],
        compiler_params=params(40),
        cost_estimate=pl.CostEstimate(
            flops=10**10, bytes_accessed=24 << 20, transcendentals=0
        ),
    )(*args)


def close_kernel(me_ref, hist_ref, out_ref):
    slots, per = out_ref.shape[0], out_ref.shape[1]
    levels, k_out, tile = hist_ref.shape[1:]
    me = me_ref[0]

    def step(i, carry):
        slot = i // per
        at = i % per
        block = (slot ^ me) * per + at
        above = hist_ref[block]
        below = jnp.concatenate(
            [above[1:], jnp.zeros((1, k_out, tile), jnp.float32)], axis=0
        )
        out_ref[slot, at] = (above - below).reshape(levels * k_out, tile).astype(BF16)
        return carry

    lax.fori_loop(0, slots * per, step, 0)


def close(me, hist, slots):
    blocks, levels, k_out, tile = hist.shape
    return pl.pallas_call(
        close_kernel,
        out_shape=jax.ShapeDtypeStruct((slots, blocks // slots, levels * k_out, tile), BF16),
        in_specs=[spec(SMEM), spec(VMEM)],
        out_specs=spec(VMEM),
        compiler_params=params(24),
    )(me, hist)


def finish_kernel(k_out, *refs):
    parts, out_ref, scratch = refs[:-2], refs[-2], refs[-1]
    blocks, rows, tile = parts[0].shape
    levels = rows // k_out
    for b in range(blocks):
        total = parts[0][b].astype(jnp.float32)
        for part in parts[1:]:
            total = total + part[b].astype(jnp.float32)
        scratch[...] = total
        for k in range(k_out):
            out_ref[k, :, b * tile : (b + 1) * tile] = scratch[pl.ds(k, levels, stride=k_out), :]


def finish(parts, k_out):
    blocks, rows, tile = parts[0].shape
    return pl.pallas_call(
        functools.partial(finish_kernel, k_out),
        out_shape=jax.ShapeDtypeStruct((k_out, rows // k_out, blocks * tile), jnp.float32),
        in_specs=[spec(VMEM)] * len(parts),
        out_specs=spec(VMEM),
        scratch_shapes=[VMEM((rows, tile), jnp.float32)],
        compiler_params=params(16),
    )(*parts)


def reduce_rows(slots, k_out, axis):
    n = slots.shape[0]
    parts = {p: [slots[p]] for p in range(n)}
    bit = 1
    while bit < n:
        for p in sorted((p for p in parts if p & bit), reverse=True):
            have = parts.pop(p)
            if len(have) > 1:
                value = functools.reduce(jnp.add, [x.astype(jnp.float32) for x in have])
                value = value.astype(BF16)
            else:
                value = have[0]
            moved = lax.ppermute(value, axis, [(i, i ^ bit) for i in range(n)])
            parts[p ^ bit].append(moved)
        bit *= 2
    return finish(parts[0], k_out)


def shards(tile_values, tile_row, tile_block, tile_count, tile_owner, cut_index, gradients):
    owners = lax.axis_size("feat")
    row_groups = lax.axis_size("rows")
    tile_dev, tile = tile_values.shape[:2]
    levels = cut_index.shape[0] + 1
    k_out, rows_dev = gradients.shape
    row_blocks = rows_dev // tile
    fb_dev = cut_index.shape[1] // tile
    per_tile = tile // ROWS_G
    capacity = max(2, 2 * tile_dev // owners) * per_tile
    static = [capacity // 6] * 4
    turn = capacity // 12
    left = capacity - sum(static)

    owner = tile_owner[:, 0]
    meta = jnp.stack(
        [owner, tile_count // tile, tile_count % tile, tile_block, tile_row], axis=0
    )
    meta = jnp.pad(meta, ((0, ROWS_G - meta.shape[0]), (0, tile - tile_dev))).astype(BF16)
    rows_first = jnp.transpose(gradients.reshape(k_out, row_blocks, tile), (1, 0, 2))
    rows_first = rows_first.reshape(row_blocks * k_out // ROWS_G, ROWS_G, tile)
    head = jnp.concatenate([rows_first, meta[None]], axis=0)
    skip = head.shape[0]

    sent = pack(owner, tile_count, tile_values, head, static + [left], (owners, capacity))

    n = 2 * cut_index + (1 - 10 * (levels - 1))
    n = jnp.where(jnp.abs(n) > 256, n - 1, n)
    cuts = (n.astype(jnp.float32) / 128.0).astype(BF16)
    cuts = jnp.concatenate([jnp.full((1, fb_dev * tile), -500.0, BF16), cuts], axis=0)
    cuts = jnp.transpose(cuts.reshape(levels, fb_dev, tile), (1, 0, 2))
    cuts = jnp.broadcast_to(cuts[:, :, None, :], (fb_dev, levels, ROWS_G, tile))

    def exchange(x):
        return lax.all_to_all(x, "feat", split_axis=0, concat_axis=0, tiled=True)

    got = [exchange(x) for x in sent[:-1]]
    known = got[0][:, skip - 1, :5, :tile_dev].astype(jnp.int32)
    grads = got[0][:, : skip - 1].reshape(owners * row_blocks, k_out, tile)
    nothing = jnp.zeros_like(grads)
    grads = jnp.stack(
        [jnp.concatenate([grads, nothing], axis=1), jnp.concatenate([nothing, grads], axis=1)],
        axis=0,
    )
    me = lax.axis_index("feat")
    room = -(-(owners * capacity // per_tile + 2) // 128) * 128

    def listed(low, size):
        window = jnp.stack([me, low, low + size]).astype(jnp.int32)
        return list_tiles(window, known, tile, row_blocks, room)

    hist = None
    low = 0
    for number, size in enumerate(static):
        entries, total = listed(low, size)
        hist = add_tiles(
            hist, entries, total, got[number], grads, cuts, skip if number == 0 else 0, k_out
        )
        low += size
    turns = (total[1] - low + turn - 1) // turn

    def more(carry):
        return carry[0] < turns

    def step(carry):
        r, hist = carry
        piece = lax.dynamic_slice_in_dim(sent[-1], r * turn, turn, axis=1)
        entries, total = listed(low + r * turn, turn)
        hist = add_tiles(hist, entries, total, exchange(piece), grads, cuts, 0, k_out)
        return r + 1, hist

    _, hist = lax.while_loop(more, step, (jnp.int32(0), hist))
    slots = close(lax.axis_index("rows").astype(jnp.int32)[None], hist, row_groups)
    return reduce_rows(slots, k_out, "rows")


def solution(mesh):
    placed = (
        P(("grp", "feat", "rows"), None, None),
        P(("grp", "feat", "rows")),
        P(("grp", "feat", "rows")),
        P(("grp", "feat", "rows")),
        P(("grp", "feat", "rows"), None),
        P(None, ("grp", "feat")),
        P(None, ("grp", "feat", "rows")),
    )
    return jax.shard_map(
        shards,
        mesh=mesh,
        in_specs=placed,
        out_specs=P(None, None, ("grp", "feat", "rows")),
        check_vma=False,
    )
```

```python
import functools

import jax
import jax.numpy as jnp
from jax import lax
from jax.experimental import pallas as pl
from jax.experimental.pallas import tpu as pltpu
from jax.sharding import PartitionSpec as P

ROWS_G = 16
VMEM = pltpu.VMEM
SMEM = pltpu.SMEM
ANY = pl.ANY
BF16 = jnp.bfloat16
INFO = 6
PACK_MIB = 56


def params(mib):
    return pltpu.CompilerParams(vmem_limit_bytes=mib << 20)


def spec(space):
    return pl.BlockSpec(memory_space=space)


def cost(flops, mib):
    return pl.CostEstimate(flops=flops, bytes_accessed=mib << 20, transcendentals=0)


def log2(n):
    assert n & (n - 1) == 0
    return n.bit_length() - 1


def shifted(x, n):
    return lax.shift_right_logical(x, jnp.int32(log2(n)))


def wrapped(x, n):
    return jnp.where(x < 0, x + n, x)


def as_bf16(x):
    return x.astype(jnp.float32).astype(BF16)


def pack_kernel(
    sizes, unit, me_ref, owner_ref, count_ref, block_ref, row_ref, grads_hbm, values_hbm, *rest
):
    number = len(sizes)
    slots, lanes = rest[-3].shape[0], rest[-3].shape[2]
    outs, infos = rest[: number * slots], rest[number * slots : (number + 1) * slots]
    scratch, values, heads, grads, info, cursor, sem = rest[(number + 1) * slots :]
    tiles, tile = values.shape[0], values.shape[1]
    per_tile = tile // ROWS_G
    k_out, row_blocks = grads.shape[0], grads.shape[1] // tile
    parts = 4 if tiles % 4 == 0 else 1
    span = tiles // parts
    loads = [
        pltpu.make_async_copy(
            values_hbm.at[pl.ds(i * span, span)], values.at[pl.ds(i * span, span)], sem.at[i]
        )
        for i in range(parts)
    ] + [pltpu.make_async_copy(grads_hbm, grads, sem.at[parts])]
    for load in loads:
        load.start()
    me = me_ref[0]
    units = sum(sizes) // unit
    for d in range(slots):
        cursor[0, d] = 0
        cursor[1, d] = 0
        for u in range(units + 1):
            info[d, 4, u] = lanes
            info[d, 5, u] = lanes
    for i in range(parts):
        loads[i].wait()

        def place(t, carry):
            d = wrapped(owner_ref[t] - me, slots)
            at, n = cursor[0, d], cursor[1, d]
            count = count_ref[t]
            end = at + shifted(count + (ROWS_G * tile - 1), ROWS_G * tile)
            cursor[0, d] = end
            cursor[1, d] = n + 1
            scratch[d, pl.ds(at, per_tile)] = values[t].reshape(per_tile, ROWS_G, tile)
            info[d, 0, n] = at
            info[d, 1, n] = count
            info[d, 2, n] = block_ref[t]
            info[d, 3, n] = row_ref[t]
            u = shifted(end - 1, unit)
            info[d, 4, jnp.where(u * unit >= at, u, lanes - 3)] = n
            u = shifted(end, unit)
            info[d, 5, jnp.where(u * unit > at, u, lanes - 3)] = n + 1
            return carry

        lax.fori_loop(i * span, (i + 1) * span, place, 0)
    most = cursor[0, 0]
    for d in range(1, slots):
        most = jnp.maximum(most, cursor[0, d])
    for d in range(slots):
        info[d, 4, lanes - 2] = cursor[1, d]
        info[d, 4, lanes - 1] = most
    loads[parts].wait()
    lines = [grads[:, b * tile : (b + 1) * tile] for b in range(row_blocks)]
    heads[...] = jnp.concatenate(lines, axis=0).reshape(heads.shape)
    copies = []
    start, at = 0, parts + 1
    for c, size in enumerate(sizes):
        skip = heads.shape[0] if c == 0 else 0
        for d in range(slots):
            out = outs[c * slots + d]
            pairs = [(scratch.at[d, pl.ds(start, size)], out.at[pl.ds(skip, size)])]
            if skip:
                pairs += [(heads, out.at[pl.ds(0, skip)]), (info.at[d], infos[d])]
            for source, target in pairs:
                copies.append(pltpu.make_async_copy(source, target, sem.at[at]))
                at += 1
        start += size
    for copy in copies:
        copy.start()
    for copy in copies:
        copy.wait()


def pack(me, owner, count, block, row, grads, values, sizes, unit, slots):
    tiles, tile = values.shape[0], values.shape[1]
    room = sum(sizes)
    lanes = 128
    assert max(2, 2 * tiles // slots) < lanes - 3 and room // unit < lanes - 3
    head = grads.size // (ROWS_G * tile)
    shapes = [
        jax.ShapeDtypeStruct((size + (head if number == 0 else 0), ROWS_G, tile), BF16)
        for number, size in enumerate(sizes)
        for _ in range(slots)
    ] + [jax.ShapeDtypeStruct((INFO, lanes), jnp.int32)] * slots
    outs = pl.pallas_call(
        functools.partial(pack_kernel, sizes, unit),
        out_shape=shapes,
        in_specs=[spec(SMEM)] * 5 + [spec(ANY)] * 2,
        out_specs=[spec(ANY)] * len(shapes),
        scratch_shapes=[
            VMEM((slots, room, ROWS_G, tile), BF16),
            VMEM(values.shape, BF16),
            VMEM((head, ROWS_G, tile), BF16),
            VMEM(grads.shape, BF16),
            SMEM((slots, INFO, lanes), jnp.int32),
            SMEM((2, slots), jnp.int32),
            pltpu.SemaphoreType.DMA((5 + (len(sizes) + 2) * slots,)),
        ],
        compiler_params=params(PACK_MIB),
        cost_estimate=cost(0, 8),
    )(me, owner, count, block, row, grads, values)
    pieces = [list(outs[i * slots : (i + 1) * slots]) for i in range(len(sizes))]
    return pieces, list(outs[-slots:]), head


def hist_kernel(kind, skip, senders, unit, row_blocks, which_ref, info_ref, *refs):
    first, last = kind
    got_refs, (grads_ref, cuts_ref), refs = (
        refs[:senders],
        refs[senders : senders + 2],
        refs[senders + 2 :],
    )
    if not first:
        before_ref, refs = refs[0], refs[1:]
    if last:
        more_ref, out_ref, hist_ref, got, sem, extra = refs
    else:
        hist_ref, got, sem = refs
    length, tile = got_refs[0].shape[0] - skip, got_refs[0].shape[2]
    per_tile = tile // ROWS_G
    blocks, levels = cuts_ref.shape[:2]
    k_out, lanes = hist_ref.shape[2], info_ref.shape[2]
    low = which_ref[0]
    copies = [
        pltpu.make_async_copy(
            got_refs[s].at[pl.ds(skip, length)],
            got.at[pl.ds(per_tile + s * length, length)],
            sem.at[s],
        )
        for s in range(senders)
    ]
    for copy in copies:
        copy.start()

    def clear(b, carry):
        hist_ref[b] = jnp.zeros(hist_ref.shape[1:], jnp.float32)
        return carry

    def keep(b, carry):
        hist_ref[b] = before_ref[b]
        return carry

    if first:
        lax.fori_loop(0, blocks, clear, 0)
    else:
        fresh = which_ref[3] > 0
        lax.fori_loop(0, jnp.where(fresh, blocks, 0), clear, 0)
        lax.fori_loop(0, jnp.where(fresh, 0, blocks), keep, 0)
    for copy in copies:
        copy.wait()
    row = as_bf16(lax.broadcasted_iota(jnp.int32, (tile, tile), 0))
    lane = as_bf16(lax.broadcasted_iota(jnp.int32, (tile, tile), 1))
    one, zero = jnp.ones((tile, tile), BF16), jnp.zeros((tile, tile), BF16)
    per = ROWS_G * tile

    def load(s, i, end):
        at, block = info_ref[s, 0, i], info_ref[s, 2, i]
        count = jnp.where(i < end, info_ref[s, 1, i], 0)
        count = jnp.minimum(count, (low + length - at) * per)
        start = per_tile + s * length + at - low
        values = got[pl.ds(start, per_tile)].reshape(tile, tile)
        whole = as_bf16(shifted(count, tile))
        part = as_bf16(count & (tile - 1))
        above = as_bf16((low - at) * ROWS_G)
        live = ((row < whole) | ((row == whole) & (lane < part))) & (row >= above)
        values = jnp.where(live, values, jnp.full_like(values, -1000.0))
        return block, values, s * row_blocks + info_ref[s, 3, i]

    def sender(s, carry):
        tiles = info_ref[s, 4, lanes - 2]
        begin = jnp.minimum(info_ref[s, 4, shifted(low, unit)], tiles)
        end = jnp.minimum(info_ref[s, 5, shifted(low + length, unit)], tiles)

        def pair(p, carry):
            i = begin + 2 * p
            block_a, va, line_a = load(s, i, end)
            block_b, vb, line_b = load(s, jnp.minimum(i + 1, end - 1), jnp.where(i + 1 < end, end, 0))
            left = jnp.concatenate([grads_ref[0, line_a], grads_ref[1, line_b]], axis=1)
            for c in range(0, levels, 2):
                columns = []
                for d in (c, c + 1):
                    cut_a = jnp.broadcast_to(cuts_ref[block_a, d : d + 1], (tile, tile))
                    cut_b = jnp.broadcast_to(cuts_ref[block_b, d : d + 1], (tile, tile))
                    columns.append(
                        jnp.concatenate(
                            [
                                jnp.where(va > cut_a.astype(BF16), one, zero),
                                jnp.where(vb > cut_b.astype(BF16), one, zero),
                            ],
                            axis=0,
                        )
                    )
                sums = jnp.dot(
                    left, jnp.concatenate(columns, axis=1), preferred_element_type=jnp.float32
                )
                hist_ref[block_a, c] += sums[:k_out, :tile]
                hist_ref[block_a, c + 1] += sums[:k_out, tile:]
                hist_ref[block_b, c] += sums[k_out:, :tile]
                hist_ref[block_b, c + 1] += sums[k_out:, tile:]
            return carry

        lax.fori_loop(0, shifted(jnp.maximum(end - begin, 0) + 1, 2), pair, 0)
        return carry

    lax.fori_loop(0, senders, sender, 0)
    if not last:
        return

    @pl.when(which_ref[1] > 0)
    def _():
        def add(b, carry):
            copy = pltpu.make_async_copy(more_ref.at[b], extra, sem.at[senders])
            copy.start()
            copy.wait()
            hist_ref[b] += extra[...]
            return carry

        lax.fori_loop(0, blocks, add, 0)

    slots, per_slot = out_ref.shape[0], out_ref.shape[1]
    me = which_ref[2]

    def step(i, carry):
        for slot in range(slots):
            above = hist_ref[(slot ^ me) * per_slot + i]
            below = jnp.concatenate(
                [above[1:], jnp.zeros((1, k_out, tile), jnp.float32)], axis=0
            )
            out_ref[slot, i] = (above - below).reshape(levels * k_out, tile).astype(BF16)
        return carry

    lax.fori_loop(0, per_slot, step, 0)


def add_tiles(hist, which, info, got, grads, cuts, skip, unit, slots=0, more=None):
    first, last = hist is None, slots > 0
    senders, length, tile = len(got), got[0].shape[0] - skip, got[0].shape[2]
    blocks, levels = cuts.shape[0], cuts.shape[1]
    k_out = grads.shape[2] // 2
    args = [which, info, *got, grads, cuts]
    specs = [spec(SMEM)] * 2 + [spec(ANY)] * senders + [spec(VMEM)] * 2
    whole = jax.ShapeDtypeStruct((blocks, levels, k_out, tile), jnp.float32)
    outs, aliases = [whole], {}
    if last:
        outs = [jax.ShapeDtypeStruct((slots, blocks // slots, levels * k_out, tile), BF16), whole]
    if not first:
        aliases = {len(args): len(outs) - 1}
        args.append(hist)
        specs.append(spec(VMEM))
    if last:
        args.append(more)
        specs.append(spec(ANY))
    result = pl.pallas_call(
        functools.partial(
            hist_kernel, (first, last), skip, senders, unit, grads.shape[1] // senders
        ),
        out_shape=outs,
        in_specs=specs,
        out_specs=[spec(VMEM)] * len(outs),
        scratch_shapes=[
            VMEM((senders * length + 2 * (tile // ROWS_G), ROWS_G, tile), BF16),
            pltpu.SemaphoreType.DMA((senders + 1,)),
        ]
        + ([VMEM(whole.shape[1:], jnp.float32)] if last else []),
        input_output_aliases=aliases,
        compiler_params=params(28),
        cost_estimate=cost(10**10, 24),
    )(*args)
    return result[0]


def unwritten(shape):
    return pl.pallas_call(
        lambda out_ref: None,
        out_shape=jax.ShapeDtypeStruct(shape, jnp.float32),
        out_specs=spec(ANY),
        compiler_params=params(PACK_MIB),
    )()


def finish_kernel(k_out, *refs):
    parts, out_ref, scratch = refs[:-2], refs[-2], refs[-1]
    blocks, rows, tile = parts[0].shape
    levels = rows // k_out
    for b in range(blocks):
        total = parts[0][b].astype(jnp.float32)
        for part in parts[1:]:
            total = total + part[b].astype(jnp.float32)
        scratch[...] = total
        for k in range(k_out):
            out_ref[k, :, b * tile : (b + 1) * tile] = scratch[pl.ds(k, levels, stride=k_out), :]


def finish(parts, k_out):
    blocks, rows, tile = parts[0].shape
    return pl.pallas_call(
        functools.partial(finish_kernel, k_out),
        out_shape=jax.ShapeDtypeStruct((k_out, rows // k_out, blocks * tile), jnp.float32),
        in_specs=[spec(VMEM)] * len(parts),
        out_specs=spec(VMEM),
        scratch_shapes=[VMEM((rows, tile), jnp.float32)],
        compiler_params=params(16),
    )(*parts)


def reduce_rows(slots, k_out, axis):
    n = slots.shape[0]
    parts = {p: [slots[p]] for p in range(n)}
    bit = 1
    while bit < n:
        for p in sorted((p for p in parts if p & bit), reverse=True):
            have = parts.pop(p)
            if len(have) > 1:
                value = functools.reduce(jnp.add, [x.astype(jnp.float32) for x in have])
                value = value.astype(BF16)
            else:
                value = have[0]
            moved = lax.ppermute(value, axis, [(i, i ^ bit) for i in range(n)])
            parts[p ^ bit].append(moved)
        bit *= 2
    return finish(parts[0], k_out)


def shards(tile_values, tile_row, tile_block, tile_count, tile_owner, cut_index, gradients):
    owners = lax.axis_size("feat")
    row_groups = lax.axis_size("rows")
    tile_dev, tile = tile_values.shape[:2]
    levels = cut_index.shape[0] + 1
    k_out, rows_dev = gradients.shape
    row_blocks = rows_dev // tile
    fb_dev = cut_index.shape[1] // tile
    per_tile = tile // ROWS_G
    capacity = max(2, 2 * tile_dev // owners) * per_tile
    static = [capacity // 12 * i for i in (1, 2, 2, 2, 1)]
    turn = max(per_tile, capacity // 12)
    left = -(-(capacity - sum(static)) // turn) * turn
    me = lax.axis_index("feat").astype(jnp.int32)
    sent, infos, skip = pack(
        me[None], tile_owner[:, 0], tile_count, tile_block, tile_row, gradients, tile_values,
        static + [left], turn, owners,
    )

    n = 2 * cut_index + (1 - 10 * (levels - 1))
    n = jnp.where(jnp.abs(n) > 256, n - 1, n)
    cuts = n.astype(jnp.float32) / 128.0
    cuts = jnp.concatenate([jnp.full((1, fb_dev * tile), -512.0, jnp.float32), cuts], axis=0)
    cuts = jnp.transpose(cuts.reshape(levels, fb_dev, tile), (1, 0, 2))

    def exchange(pieces):
        moved = [
            lax.ppermute(pieces[d], "feat", [(i, (i + d) % owners) for i in range(owners)])
            for d in range(1, owners)
        ]
        return [pieces[0]] + moved

    info = jnp.stack(exchange(infos), axis=0)
    got = []
    for number in range(len(static)):
        pieces = sent[number]
        if number > 1:
            got[number - 2], pieces = lax.optimization_barrier((got[number - 2], pieces))
        got.append(exchange(pieces))

    grads = jnp.stack([x[:skip] for x in got[0]], axis=0)
    grads = grads.reshape(owners * row_blocks, k_out, tile)
    nothing = jnp.zeros_like(grads)
    grads = jnp.stack(
        [jnp.concatenate([grads, nothing], axis=1), jnp.concatenate([nothing, grads], axis=1)],
        axis=0,
    )
    mine = lax.axis_index("rows").astype(jnp.int32)

    most = jnp.max(info[:, 4, -1])
    turns = (most - sum(static) + turn - 1) // turn

    def which(low, fresh=0):
        return jnp.stack([jnp.asarray(x, jnp.int32) for x in (low, turns, mine, fresh)])

    def more(carry):
        return carry[0] < turns

    def step(carry):
        r, hist = carry
        pieces = [lax.dynamic_slice_in_dim(x, r * turn, turn, axis=0) for x in sent[-1]]
        hist = add_tiles(
            hist,
            which(sum(static) + r * turn, r == 0),
            info,
            exchange(pieces),
            grads,
            cuts,
            0,
            turn,
        )
        return r + 1, hist

    extra = unwritten((fb_dev, levels, k_out, tile))
    _, extra = lax.while_loop(more, step, (jnp.int32(0), extra))
    extra, grads = lax.optimization_barrier((extra, grads))
    hist, low = None, 0
    for number, size in enumerate(static):
        last = {"slots": row_groups, "more": extra} if number == len(static) - 1 else {}
        hist = add_tiles(
            hist, which(low), info, got[number], grads, cuts, 0 if number else skip, turn, **last
        )
        low += size
    return reduce_rows(hist, k_out, "rows")


def solution(mesh):
    placed = (
        P(("grp", "feat", "rows"), None, None),
        P(("grp", "feat", "rows")),
        P(("grp", "feat", "rows")),
        P(("grp", "feat", "rows")),
        P(("grp", "feat", "rows"), None),
        P(None, ("grp", "feat")),
        P(None, ("grp", "feat", "rows")),
    )
    return jax.shard_map(
        shards,
        mesh=mesh,
        in_specs=placed,
        out_specs=P(None, None, ("grp", "feat", "rows")),
        check_vma=False,
    )
```

```python
import functools

import jax
import jax.numpy as jnp
from jax import lax
from jax.experimental import pallas as pl
from jax.experimental.pallas import tpu as pltpu
from jax.sharding import PartitionSpec as P

ROWS_G = 8
PACKED = 16
VMEM = pltpu.VMEM
SMEM = pltpu.SMEM
ANY = pl.ANY
BF16 = jnp.bfloat16
INFO = 8
CHUNKS = (2, 6, 7, 7, 5, 4)
TURN = 4
AT_ONCE = 4
DIGIT = 256
PACK_MIB = 56


def params(mib):
    return pltpu.CompilerParams(vmem_limit_bytes=mib << 20)


def spec(space):
    return pl.BlockSpec(memory_space=space)


def cost(flops, mib):
    return pl.CostEstimate(flops=flops, bytes_accessed=mib << 20, transcendentals=0)


def log2(n):
    assert n & (n - 1) == 0
    return n.bit_length() - 1


def shifted(x, n):
    return lax.shift_right_logical(x, jnp.int32(log2(n)))


def wrapped(x, n):
    return jnp.where(x < 0, x + n, x)


def as_bf16(x):
    return x.astype(jnp.float32).astype(BF16)


def pack_kernel(
    sizes, unit, me_ref, owner_ref, count_ref, block_ref, row_ref, grads_hbm, values_hbm, *rest
):
    number = len(sizes)
    slots, lanes = rest[-4].shape[0], rest[-4].shape[2]
    outs = rest[: number * slots]
    scratch, values, heads, grads, info, lines, cursor, sem = rest[number * slots :]
    tiles, per_tile, _, tile = values.shape
    k_out, row_blocks = grads.shape[0], grads.shape[1] // tile
    parts = 4 if tiles % 4 == 0 else 1
    span = tiles // parts
    loads = [
        pltpu.make_async_copy(
            values_hbm.at[pl.ds(i * span, span)], values.at[pl.ds(i * span, span)], sem.at[i]
        )
        for i in range(parts)
    ] + [pltpu.make_async_copy(grads_hbm, grads, sem.at[parts])]
    for load in loads:
        load.start()
    me = me_ref[0]
    units = sum(sizes) // unit
    for d in range(slots):
        cursor[0, d] = 0
        cursor[1, d] = 0
        for u in range(units + 1):
            info[d, 4, u] = lanes
            info[d, 5, u] = lanes
    for i in range(parts):
        loads[i].wait()

        def place(t, carry):
            d = wrapped(owner_ref[t] - me, slots)
            at, n = cursor[0, d], cursor[1, d]
            count = count_ref[t]
            end = at + shifted(count + (ROWS_G * tile - 1), ROWS_G * tile)
            cursor[0, d] = end
            cursor[1, d] = n + 1
            scratch[d, pl.ds(at, per_tile)] = values[t]
            info[d, 0, n] = at
            info[d, 1, n] = count
            info[d, 2, n] = block_ref[t]
            info[d, 3, n] = row_ref[t]
            u = shifted(end - 1, unit)
            info[d, 4, jnp.where(u * unit >= at, u, lanes - 3)] = n
            u = shifted(end, unit)
            info[d, 5, jnp.where(u * unit > at, u, lanes - 3)] = n + 1
            return carry

        lax.fori_loop(i * span, (i + 1) * span, place, 0)
    most = cursor[0, 0]
    for d in range(1, slots):
        most = jnp.maximum(most, cursor[0, d])
    for d in range(slots):
        info[d, 4, lanes - 2] = cursor[1, d]
        info[d, 4, lanes - 1] = most
    listed = pltpu.make_async_copy(info, lines, sem.at[parts + 1])
    listed.start()
    loads[parts].wait()
    stack = [grads[:, b * tile : (b + 1) * tile] for b in range(row_blocks)]
    listed.wait()
    for d in range(slots):
        for b in range(row_blocks):
            heads[d, b] = stack[b]
        heads[d, row_blocks] = as_bf16(shifted(lines[d], DIGIT))
        heads[d, row_blocks + 1] = as_bf16(lines[d] & (DIGIT - 1))
    copies = []
    start, at = 0, parts + 2
    for c, size in enumerate(sizes):
        skip = heads.shape[1] if c == 0 else 0
        for d in range(slots):
            out = outs[c * slots + d]
            pairs = [(scratch.at[d, pl.ds(start, size)], out.at[pl.ds(skip, size)])]
            if skip:
                pairs += [(heads.at[d], out.at[pl.ds(0, skip)])]
            for source, target in pairs:
                copies.append(pltpu.make_async_copy(source, target, sem.at[at]))
                at += 1
        start += size
    always, rare = copies[:-slots], copies[-slots:]
    for copy in always:
        copy.start()

    @pl.when(most > start - sizes[-1])
    def _():
        for copy in rare:
            copy.start()
        for copy in rare:
            copy.wait()

    for copy in always:
        copy.wait()


def pack(me, owner, count, block, row, grads, values, sizes, unit, slots):
    tiles, tile = values.shape[0], values.shape[1]
    values = values.reshape(tiles, tile // ROWS_G, ROWS_G, tile)
    room = sum(sizes)
    lanes = 128
    assert max(2, 2 * tiles // slots) < lanes - 3 and room // unit < lanes - 3
    assert lanes == tile and INFO == ROWS_G == grads.shape[0]
    head = grads.size // (ROWS_G * tile) + 2
    shapes = [
        jax.ShapeDtypeStruct((size + (head if number == 0 else 0), ROWS_G, tile), BF16)
        for number, size in enumerate(sizes)
        for _ in range(slots)
    ]
    outs = pl.pallas_call(
        functools.partial(pack_kernel, sizes, unit),
        out_shape=shapes,
        in_specs=[spec(SMEM)] * 5 + [spec(ANY)] * 2,
        out_specs=[spec(ANY)] * len(shapes),
        scratch_shapes=[
            VMEM((slots, room, ROWS_G, tile), BF16),
            VMEM(values.shape, BF16),
            VMEM((slots, head, ROWS_G, tile), BF16),
            VMEM(grads.shape, BF16),
            SMEM((slots, INFO, lanes), jnp.int32),
            VMEM((slots, INFO, lanes), jnp.int32),
            SMEM((2, slots), jnp.int32),
            pltpu.SemaphoreType.DMA((6 + (len(sizes) + 1) * slots,)),
        ],
        compiler_params=params(PACK_MIB),
        cost_estimate=cost(0, 8),
    )(me, owner, count, block, row, grads, values)
    pieces = [list(outs[i * slots : (i + 1) * slots]) for i in range(len(sizes))]
    return pieces, head


def hist_kernel(kind, skip, senders, unit, row_blocks, which_ref, info_ref, *refs):
    first, last = kind
    got_refs, (grads_ref, cuts_ref), refs = (
        refs[:senders],
        refs[senders : senders + 2],
        refs[senders + 2 :],
    )
    if not first:
        before_ref, refs = refs[0], refs[1:]
    if last:
        more_ref, out_ref, hist_ref, got, list_ref, sem, extra = refs
    else:
        hist_ref, got, list_ref, sem = refs
    length, tile = got_refs[0].shape[0] - skip, got_refs[0].shape[2]
    per_tile = tile // ROWS_G
    blocks, levels = cuts_ref.shape[:2]
    k_out, lanes = hist_ref.shape[2], info_ref.shape[2]
    low = which_ref[0]
    copies = [
        pltpu.make_async_copy(
            got_refs[s].at[pl.ds(skip, length)],
            got.at[pl.ds(per_tile + s * length, length)],
            sem.at[s],
        )
        for s in range(senders)
    ]
    for copy in copies:
        copy.start()
    found = jnp.int32(0)
    for s in range(senders):
        tiles = info_ref[s, 4, lanes - 2]
        begin = jnp.minimum(info_ref[s, 4, shifted(low, unit)], tiles)
        end = jnp.minimum(info_ref[s, 5, shifted(low + length, unit)], tiles)

        def put(i, at, s=s):
            list_ref[at] = s * lanes + i
            return at + 1

        found = lax.fori_loop(begin, end, put, found)
    for i in range(AT_ONCE - 1):
        list_ref[found + i] = -1

    def clear(b, carry):
        hist_ref[b] = jnp.zeros(hist_ref.shape[1:], jnp.float32)
        return carry

    def keep(b, carry):
        hist_ref[b] = before_ref[b]
        return carry

    if first:
        lax.fori_loop(0, blocks, clear, 0)
    else:
        fresh = which_ref[3] > 0
        lax.fori_loop(0, jnp.where(fresh, blocks, 0), clear, 0)
        lax.fori_loop(0, jnp.where(fresh, 0, blocks), keep, 0)
    for copy in copies:
        copy.wait()
    row = as_bf16(lax.broadcasted_iota(jnp.int32, (tile, tile), 0))
    lane = as_bf16(lax.broadcasted_iota(jnp.int32, (tile, tile), 1))
    one, zero = jnp.ones((tile, tile), BF16), jnp.zeros((tile, tile), BF16)
    per = ROWS_G * tile

    def entry(p):
        e = list_ref[p]
        s, i, real = e >> log2(lanes), e & (lanes - 1), e >= 0
        at = jnp.where(real, info_ref[s & (senders - 1), 0, i], low)
        block = jnp.where(real, info_ref[s & (senders - 1), 2, i], 0)
        count = jnp.where(real, info_ref[s & (senders - 1), 1, i], 0)
        line = jnp.where(real, s * row_blocks + info_ref[s & (senders - 1), 3, i], 0)
        start = per_tile + jnp.where(real, s, 0) * length + at - low
        return start, block, jnp.minimum(count, (low + length - at) * per), (low - at) * ROWS_G, line

    def load(p):
        start, block, count, above, line = entry(p)
        values = got[pl.ds(start, per_tile)].reshape(tile, tile)
        whole = as_bf16(shifted(count, tile))
        part = as_bf16(count & (tile - 1))
        live = ((row < whole) | ((row == whole) & (lane < part))) & (row >= as_bf16(above))
        values = jnp.where(live, values, jnp.full_like(values, -1000.0))
        return block, values, line

    def pair(p):
        block_a, va, line_a = load(p)
        block_b, vb, line_b = load(p + 1)
        left = jnp.concatenate([grads_ref[0, line_a], grads_ref[1, line_b]], axis=1)
        for c in range(0, levels, 2):
            columns = []
            for d in (c, c + 1):
                cut_a = jnp.broadcast_to(cuts_ref[block_a, d : d + 1], (tile, tile))
                cut_b = jnp.broadcast_to(cuts_ref[block_b, d : d + 1], (tile, tile))
                columns.append(
                    jnp.concatenate(
                        [
                            jnp.where(va > cut_a.astype(BF16), one, zero),
                            jnp.where(vb > cut_b.astype(BF16), one, zero),
                        ],
                        axis=0,
                    )
                )
            sums = jnp.dot(
                left, jnp.concatenate(columns, axis=1), preferred_element_type=jnp.float32
            )
            hist_ref[block_a, c] += sums[:k_out, :tile]
            hist_ref[block_a, c + 1] += sums[:k_out, tile:]
            hist_ref[block_b, c] += sums[k_out:, :tile]
            hist_ref[block_b, c + 1] += sums[k_out:, tile:]

    def group(i, carry):
        for j in range(0, AT_ONCE, 2):
            pair(AT_ONCE * i + j)
        return carry

    lax.fori_loop(0, (found + AT_ONCE - 1) >> log2(AT_ONCE), group, 0)
    if not last:
        return

    @pl.when(which_ref[1] > 0)
    def _():
        def add(b, carry):
            copy = pltpu.make_async_copy(more_ref.at[b], extra, sem.at[senders])
            copy.start()
            copy.wait()
            hist_ref[b] += extra[...]
            return carry

        lax.fori_loop(0, blocks, add, 0)

    slots, per_slot = out_ref.shape[0], out_ref.shape[1]
    me = which_ref[2]

    def step(i, carry):
        for slot in range(slots):
            above = hist_ref[(slot ^ me) * per_slot + i]
            below = jnp.concatenate(
                [above[1:], jnp.zeros((1, k_out, tile), jnp.float32)], axis=0
            )
            out_ref[slot, i] = (above - below).reshape(levels * k_out, tile).astype(BF16)
        return carry

    lax.fori_loop(0, per_slot, step, 0)


def add_tiles(hist, which, info, got, grads, cuts, skip, unit, slots=0, more=None):
    first, last = hist is None, slots > 0
    senders, length, tile = len(got), got[0].shape[0] - skip, got[0].shape[2]
    blocks, levels = cuts.shape[0], cuts.shape[1]
    k_out = grads.shape[2] // 2
    args = [which, info, *got, grads, cuts]
    specs = [spec(SMEM)] * 2 + [spec(ANY)] * senders + [spec(VMEM)] * 2
    whole = jax.ShapeDtypeStruct((blocks, levels, k_out, tile), jnp.float32)
    outs, aliases = [whole], {}
    if last:
        outs = [jax.ShapeDtypeStruct((slots, blocks // slots, levels * k_out, tile), BF16), whole]
    if not first:
        aliases = {len(args): len(outs) - 1}
        args.append(hist)
        specs.append(spec(VMEM))
    if last:
        args.append(more)
        specs.append(spec(ANY))
    result = pl.pallas_call(
        functools.partial(
            hist_kernel, (first, last), skip, senders, unit, grads.shape[1] // senders
        ),
        out_shape=outs,
        in_specs=specs,
        out_specs=[spec(VMEM)] * len(outs),
        scratch_shapes=[
            VMEM((senders * length + 2 * (tile // ROWS_G), ROWS_G, tile), BF16),
            SMEM((senders * (length + 1) + AT_ONCE,), jnp.int32),
            pltpu.SemaphoreType.DMA((senders + 1,)),
        ]
        + ([VMEM(whole.shape[1:], jnp.float32)] if last else []),
        input_output_aliases=aliases,
        compiler_params=params(28),
        cost_estimate=cost(10**10, 24),
    )(*args)
    return result[0]


def unwritten(shape):
    return pl.pallas_call(
        lambda out_ref: None,
        out_shape=jax.ShapeDtypeStruct(shape, jnp.float32),
        out_specs=spec(ANY),
        compiler_params=params(PACK_MIB),
    )()


def finish_kernel(k_out, *refs):
    parts, out_ref, scratch = refs[:-2], refs[-2], refs[-1]
    blocks, rows, tile = parts[0].shape
    levels = rows // k_out
    for b in range(blocks):
        total = parts[0][b].astype(jnp.float32)
        for part in parts[1:]:
            total = total + part[b].astype(jnp.float32)
        scratch[...] = total
        for k in range(k_out):
            out_ref[k, :, b * tile : (b + 1) * tile] = scratch[pl.ds(k, levels, stride=k_out), :]


def finish(parts, k_out):
    blocks, rows, tile = parts[0].shape
    return pl.pallas_call(
        functools.partial(finish_kernel, k_out),
        out_shape=jax.ShapeDtypeStruct((k_out, rows // k_out, blocks * tile), jnp.float32),
        in_specs=[spec(VMEM)] * len(parts),
        out_specs=spec(VMEM),
        scratch_shapes=[VMEM((rows, tile), jnp.float32)],
        compiler_params=params(16),
    )(*parts)


def reduce_rows(slots, k_out, axis):
    n = slots.shape[0]
    parts = {p: [slots[p]] for p in range(n)}
    bit = 1
    while bit < n:
        for p in sorted((p for p in parts if p & bit), reverse=True):
            have = parts.pop(p)
            if len(have) > 1:
                value = functools.reduce(jnp.add, [x.astype(jnp.float32) for x in have])
                value = value.astype(BF16)
            else:
                value = have[0]
            moved = lax.ppermute(value, axis, [(i, i ^ bit) for i in range(n)])
            parts[p ^ bit].append(moved)
        bit *= 2
    return finish(parts[0], k_out)


def shards(tile_values, tile_row, tile_block, tile_count, tile_owner, cut_index, gradients):
    owners = lax.axis_size("feat")
    row_groups = lax.axis_size("rows")
    tile_dev, tile = tile_values.shape[:2]
    levels = cut_index.shape[0] + 1
    k_out, rows_dev = gradients.shape
    row_blocks = rows_dev // tile
    fb_dev = cut_index.shape[1] // tile
    per_tile = tile // ROWS_G
    capacity = max(2, 2 * tile_dev // owners) * per_tile
    unit = per_tile
    units = capacity // unit
    static = [max(1, units * i // 48) * unit for i in CHUNKS]
    while sum(static) >= capacity:
        static.pop()
    turn = min(TURN, capacity // per_tile // 12 + 1) * unit
    left = -(-(capacity - sum(static)) // turn) * turn
    me = lax.axis_index("feat").astype(jnp.int32)
    sent, skip = pack(
        me[None], tile_owner[:, 0], tile_count, tile_block, tile_row, gradients, tile_values,
        static + [left], unit, owners,
    )

    n = 2 * cut_index + (1 - 10 * (levels - 1))
    n = jnp.where(jnp.abs(n) > 256, n - 1, n)
    cuts = n.astype(jnp.float32) / 128.0
    cuts = jnp.concatenate([jnp.full((1, fb_dev * tile), -512.0, jnp.float32), cuts], axis=0)
    cuts = jnp.transpose(cuts.reshape(levels, fb_dev, tile), (1, 0, 2))

    def exchange(pieces):
        moved = [
            lax.ppermute(pieces[d], "feat", [(i, (i + d) % owners) for i in range(owners)])
            for d in range(1, owners)
        ]
        return [pieces[0]] + moved

    got = []
    for number in range(len(static)):
        pieces = sent[number]
        if number > 1:
            got[number - 2], pieces = lax.optimization_barrier((got[number - 2], pieces))
        got.append(exchange(pieces))

    heads = jnp.stack([x[:skip] for x in got[0]], axis=0)
    digits = heads[:, skip - 2 :].astype(jnp.int32)
    info = digits[:, 0] * DIGIT + digits[:, 1]
    grads = heads[:, : skip - 2].reshape(owners * row_blocks, k_out, tile)
    nothing = jnp.zeros_like(grads)
    grads = jnp.stack(
        [jnp.concatenate([grads, nothing], axis=1), jnp.concatenate([nothing, grads], axis=1)],
        axis=0,
    )
    mine = lax.axis_index("rows").astype(jnp.int32)

    most = jnp.max(info[:, 4, -1])
    turns = (most - sum(static) + turn - 1) // turn

    def which(low, fresh=0):
        return jnp.stack([jnp.asarray(x, jnp.int32) for x in (low, turns, mine, fresh)])

    def more(carry):
        return carry[0] < turns

    def step(carry):
        r, hist = carry
        pieces = [lax.dynamic_slice_in_dim(x, r * turn, turn, axis=0) for x in sent[-1]]
        hist = add_tiles(
            hist,
            which(sum(static) + r * turn, r == 0),
            info,
            exchange(pieces),
            grads,
            cuts,
            0,
            unit,
        )
        return r + 1, hist

    extra = unwritten((fb_dev, levels, k_out, tile))
    _, extra = lax.while_loop(more, step, (jnp.int32(0), extra))
    extra, grads = lax.optimization_barrier((extra, grads))
    hist, low = None, 0
    for number, size in enumerate(static):
        last = {"slots": row_groups, "more": extra} if number == len(static) - 1 else {}
        hist = add_tiles(
            hist, which(low), info, got[number], grads, cuts, 0 if number else skip, unit, **last
        )
        low += size
    return reduce_rows(hist, k_out, "rows")


def solution(mesh):
    placed = (
        P(("grp", "feat", "rows"), None, None),
        P(("grp", "feat", "rows")),
        P(("grp", "feat", "rows")),
        P(("grp", "feat", "rows")),
        P(("grp", "feat", "rows"), None),
        P(None, ("grp", "feat")),
        P(None, ("grp", "feat", "rows")),
    )
    return jax.shard_map(
        shards,
        mesh=mesh,
        in_specs=placed,
        out_specs=P(None, None, ("grp", "feat", "rows")),
        check_vma=False,
    )
```

```python
import functools

import jax
import jax.numpy as jnp
from jax import lax
from jax.experimental import pallas as pl
from jax.experimental.pallas import tpu as pltpu
from jax.sharding import PartitionSpec as P

ROWS_G = 8
PACKED = 16
VMEM = pltpu.VMEM
SMEM = pltpu.SMEM
ANY = pl.ANY
BF16 = jnp.bfloat16
INFO = 8
CHUNKS = (3, 7, 6, 5, 5, 5)
TURN = 4
AT_ONCE = 8
DIGIT = 256
PACK_MIB = 56


def params(mib):
    return pltpu.CompilerParams(vmem_limit_bytes=mib << 20)


def spec(space):
    return pl.BlockSpec(memory_space=space)


def cost(flops, mib):
    return pl.CostEstimate(flops=flops, bytes_accessed=mib << 20, transcendentals=0)


def log2(n):
    assert n & (n - 1) == 0
    return n.bit_length() - 1


def shifted(x, n):
    return lax.shift_right_logical(x, jnp.int32(log2(n)))


def wrapped(x, n):
    return jnp.where(x < 0, x + n, x)


def as_bf16(x):
    return x.astype(jnp.float32).astype(BF16)


def pack_kernel(
    sizes, unit, me_ref, owner_ref, count_ref, block_ref, row_ref, grads_hbm, values_hbm, *rest
):
    number = len(sizes)
    slots, lanes = rest[-4].shape[0], rest[-4].shape[2]
    outs = rest[: number * slots]
    scratch, values, heads, grads, info, lines, cursor, sem = rest[number * slots :]
    tiles, per_tile, _, tile = values.shape
    k_out, row_blocks = grads.shape[0], grads.shape[1] // tile
    parts = 4 if tiles % 4 == 0 else 1
    span = tiles // parts
    loads = [
        pltpu.make_async_copy(
            values_hbm.at[pl.ds(i * span, span)], values.at[pl.ds(i * span, span)], sem.at[i]
        )
        for i in range(parts)
    ] + [pltpu.make_async_copy(grads_hbm, grads, sem.at[parts])]
    for load in loads:
        load.start()
    me = me_ref[0]
    units = sum(sizes) // unit
    for d in range(slots):
        cursor[0, d] = 0
        cursor[1, d] = 0
        for u in range(units + 1):
            info[d, 4, u] = lanes
            info[d, 5, u] = lanes
    for i in range(parts):
        loads[i].wait()

        def place(t, carry):
            d = wrapped(owner_ref[t] - me, slots)
            at, n = cursor[0, d], cursor[1, d]
            count = count_ref[t]
            end = at + shifted(count + (ROWS_G * tile - 1), ROWS_G * tile)
            cursor[0, d] = end
            cursor[1, d] = n + 1
            scratch[d, pl.ds(at, per_tile)] = values[t]
            info[d, 0, n] = at
            info[d, 1, n] = count
            info[d, 2, n] = block_ref[t]
            info[d, 3, n] = row_ref[t]
            u = shifted(end - 1, unit)
            info[d, 4, jnp.where(u * unit >= at, u, lanes - 3)] = n
            u = shifted(end, unit)
            info[d, 5, jnp.where(u * unit > at, u, lanes - 3)] = n + 1
            return carry

        lax.fori_loop(i * span, (i + 1) * span, place, 0)
    most = cursor[0, 0]
    for d in range(1, slots):
        most = jnp.maximum(most, cursor[0, d])
    for d in range(slots):
        info[d, 4, lanes - 2] = cursor[1, d]
        info[d, 4, lanes - 1] = most
    listed = pltpu.make_async_copy(info, lines, sem.at[parts + 1])
    listed.start()
    loads[parts].wait()
    stack = [grads[:, b * tile : (b + 1) * tile] for b in range(row_blocks)]
    listed.wait()
    for d in range(slots):
        for b in range(row_blocks):
            heads[d, b] = stack[b]
        heads[d, row_blocks] = as_bf16(shifted(lines[d], DIGIT))
        heads[d, row_blocks + 1] = as_bf16(lines[d] & (DIGIT - 1))
    copies = []
    start, at = 0, parts + 2
    for c, size in enumerate(sizes):
        skip = heads.shape[1] if c == 0 else 0
        for d in range(slots):
            out = outs[c * slots + d]
            pairs = [(scratch.at[d, pl.ds(start, size)], out.at[pl.ds(skip, size)])]
            if skip:
                pairs += [(heads.at[d], out.at[pl.ds(0, skip)])]
            for source, target in pairs:
                copies.append(pltpu.make_async_copy(source, target, sem.at[at]))
                at += 1
        start += size
    always, rare = copies[:-slots], copies[-slots:]
    for copy in always:
        copy.start()

    @pl.when(most > start - sizes[-1])
    def _():
        for copy in rare:
            copy.start()
        for copy in rare:
            copy.wait()

    for copy in always:
        copy.wait()


def pack(me, owner, count, block, row, grads, values, sizes, unit, slots):
    tiles, tile = values.shape[0], values.shape[1]
    values = values.reshape(tiles, tile // ROWS_G, ROWS_G, tile)
    room = sum(sizes)
    lanes = 128
    assert max(2, 2 * tiles // slots) < lanes - 3 and room // unit < lanes - 3
    assert lanes == tile and INFO == ROWS_G == grads.shape[0]
    head = grads.size // (ROWS_G * tile) + 2
    shapes = [
        jax.ShapeDtypeStruct((size + (head if number == 0 else 0), ROWS_G, tile), BF16)
        for number, size in enumerate(sizes)
        for _ in range(slots)
    ]
    outs = pl.pallas_call(
        functools.partial(pack_kernel, sizes, unit),
        out_shape=shapes,
        in_specs=[spec(SMEM)] * 5 + [spec(ANY)] * 2,
        out_specs=[spec(ANY)] * len(shapes),
        scratch_shapes=[
            VMEM((slots, room, ROWS_G, tile), BF16),
            VMEM(values.shape, BF16),
            VMEM((slots, head, ROWS_G, tile), BF16),
            VMEM(grads.shape, BF16),
            SMEM((slots, INFO, lanes), jnp.int32),
            VMEM((slots, INFO, lanes), jnp.int32),
            SMEM((2, slots), jnp.int32),
            pltpu.SemaphoreType.DMA((6 + (len(sizes) + 1) * slots,)),
        ],
        compiler_params=params(PACK_MIB),
        cost_estimate=cost(0, 8),
    )(me, owner, count, block, row, grads, values)
    pieces = [list(outs[i * slots : (i + 1) * slots]) for i in range(len(sizes))]
    return pieces, head


def hist_kernel(kind, skip, senders, unit, row_blocks, which_ref, info_ref, *refs):
    first, last = kind
    got_refs, (grads_ref, cuts_ref), refs = (
        refs[:senders],
        refs[senders : senders + 2],
        refs[senders + 2 :],
    )
    if not first:
        before_ref, refs = refs[0], refs[1:]
    if last:
        more_ref, out_ref, hist_ref, got, list_ref, sem, extra = refs
    else:
        hist_ref, got, list_ref, sem = refs
    length, tile = got_refs[0].shape[0] - skip, got_refs[0].shape[2]
    per_tile = tile // ROWS_G
    blocks, levels = cuts_ref.shape[:2]
    k_out, lanes = hist_ref.shape[2], info_ref.shape[2]
    low = which_ref[0]
    copies = [
        pltpu.make_async_copy(
            got_refs[s].at[pl.ds(skip, length)],
            got.at[pl.ds(per_tile + s * length, length)],
            sem.at[s],
        )
        for s in range(senders)
    ]
    for copy in copies:
        copy.start()
    found = jnp.int32(0)
    for s in range(senders):
        tiles = info_ref[s, 4, lanes - 2]
        begin = jnp.minimum(info_ref[s, 4, shifted(low, unit)], tiles)
        end = jnp.minimum(info_ref[s, 5, shifted(low + length, unit)], tiles)

        def put(i, at, s=s):
            list_ref[at] = s * lanes + i
            return at + 1

        found = lax.fori_loop(begin, end, put, found)
    list_ref[found] = -1

    def clear(b, carry):
        hist_ref[b] = jnp.zeros(hist_ref.shape[1:], jnp.float32)
        return carry

    def keep(b, carry):
        hist_ref[b] = before_ref[b]
        return carry

    if first:
        lax.fori_loop(0, blocks, clear, 0)
    else:
        fresh = which_ref[3] > 0
        lax.fori_loop(0, jnp.where(fresh, blocks, 0), clear, 0)
        lax.fori_loop(0, jnp.where(fresh, 0, blocks), keep, 0)
    for copy in copies:
        copy.wait()
    row = as_bf16(lax.broadcasted_iota(jnp.int32, (tile, tile), 0))
    lane = as_bf16(lax.broadcasted_iota(jnp.int32, (tile, tile), 1))
    one, zero = jnp.ones((tile, tile), BF16), jnp.zeros((tile, tile), BF16)
    per = ROWS_G * tile

    def entry(p):
        e = list_ref[p]
        s, i, real = e >> log2(lanes), e & (lanes - 1), e >= 0
        at = jnp.where(real, info_ref[s & (senders - 1), 0, i], low)
        block = jnp.where(real, info_ref[s & (senders - 1), 2, i], 0)
        count = jnp.where(real, info_ref[s & (senders - 1), 1, i], 0)
        line = jnp.where(real, s * row_blocks + info_ref[s & (senders - 1), 3, i], 0)
        start = per_tile + jnp.where(real, s, 0) * length + at - low
        return start, block, jnp.minimum(count, (low + length - at) * per), (low - at) * ROWS_G, line

    def load(p):
        start, block, count, above, line = entry(p)
        values = got[pl.ds(start, per_tile)].reshape(tile, tile)
        whole = as_bf16(shifted(count, tile))
        part = as_bf16(count & (tile - 1))
        live = ((row < whole) | ((row == whole) & (lane < part))) & (row >= as_bf16(above))
        values = jnp.where(live, values, jnp.full_like(values, -1000.0))
        return block, values, line

    def pair(p):
        block_a, va, line_a = load(p)
        block_b, vb, line_b = load(p + 1)
        left = jnp.concatenate([grads_ref[0, line_a], grads_ref[1, line_b]], axis=1)
        for c in range(0, levels, 2):
            columns = []
            for d in (c, c + 1):
                cut_a = jnp.broadcast_to(cuts_ref[block_a, d : d + 1], (tile, tile))
                cut_b = jnp.broadcast_to(cuts_ref[block_b, d : d + 1], (tile, tile))
                columns.append(
                    jnp.concatenate(
                        [
                            jnp.where(va > cut_a.astype(BF16), one, zero),
                            jnp.where(vb > cut_b.astype(BF16), one, zero),
                        ],
                        axis=0,
                    )
                )
            sums = jnp.dot(
                left, jnp.concatenate(columns, axis=1), preferred_element_type=jnp.float32
            )
            hist_ref[block_a, c] += sums[:k_out, :tile]
            hist_ref[block_a, c + 1] += sums[:k_out, tile:]
            hist_ref[block_b, c] += sums[k_out:, :tile]
            hist_ref[block_b, c + 1] += sums[k_out:, tile:]

    def group(i, carry):
        for j in range(0, AT_ONCE, 2):
            pair(AT_ONCE * i + j)
        return carry

    whole_groups = found >> log2(AT_ONCE)
    lax.fori_loop(0, whole_groups, group, 0)

    def single(i, carry):
        pair(2 * i)
        return carry

    lax.fori_loop(whole_groups * (AT_ONCE // 2), (found + 1) >> 1, single, 0)
    if not last:
        return

    @pl.when(which_ref[1] > 0)
    def _():
        def add(b, carry):
            copy = pltpu.make_async_copy(more_ref.at[b], extra, sem.at[senders])
            copy.start()
            copy.wait()
            hist_ref[b] += extra[...]
            return carry

        lax.fori_loop(0, blocks, add, 0)

    slots, per_slot = out_ref.shape[0], out_ref.shape[1]
    me = which_ref[2]

    def step(i, carry):
        for slot in range(slots):
            above = hist_ref[(slot ^ me) * per_slot + i]
            below = jnp.concatenate(
                [above[1:], jnp.zeros((1, k_out, tile), jnp.float32)], axis=0
            )
            out_ref[slot, i] = (above - below).reshape(levels * k_out, tile).astype(BF16)
        return carry

    lax.fori_loop(0, per_slot, step, 0)


def add_tiles(hist, which, info, got, grads, cuts, skip, unit, slots=0, more=None):
    first, last = hist is None, slots > 0
    senders, length, tile = len(got), got[0].shape[0] - skip, got[0].shape[2]
    blocks, levels = cuts.shape[0], cuts.shape[1]
    k_out = grads.shape[2] // 2
    args = [which, info, *got, grads, cuts]
    specs = [spec(SMEM)] * 2 + [spec(ANY)] * senders + [spec(VMEM)] * 2
    whole = jax.ShapeDtypeStruct((blocks, levels, k_out, tile), jnp.float32)
    outs, aliases = [whole], {}
    if last:
        outs = [jax.ShapeDtypeStruct((slots, blocks // slots, levels * k_out, tile), BF16), whole]
    if not first:
        aliases = {len(args): len(outs) - 1}
        args.append(hist)
        specs.append(spec(VMEM))
    if last:
        args.append(more)
        specs.append(spec(ANY))
    result = pl.pallas_call(
        functools.partial(
            hist_kernel, (first, last), skip, senders, unit, grads.shape[1] // senders
        ),
        out_shape=outs,
        in_specs=specs,
        out_specs=[spec(VMEM)] * len(outs),
        scratch_shapes=[
            VMEM((senders * length + 2 * (tile // ROWS_G), ROWS_G, tile), BF16),
            SMEM((senders * (length + 1) + AT_ONCE,), jnp.int32),
            pltpu.SemaphoreType.DMA((senders + 1,)),
        ]
        + ([VMEM(whole.shape[1:], jnp.float32)] if last else []),
        input_output_aliases=aliases,
        compiler_params=params(28),
        cost_estimate=cost(10**10, 24),
    )(*args)
    return result[0]


def unwritten(shape):
    return pl.pallas_call(
        lambda out_ref: None,
        out_shape=jax.ShapeDtypeStruct(shape, jnp.float32),
        out_specs=spec(ANY),
        compiler_params=params(PACK_MIB),
    )()


def finish_kernel(k_out, *refs):
    parts, out_ref, scratch = refs[:-2], refs[-2], refs[-1]
    blocks, rows, tile = parts[0].shape
    levels = rows // k_out
    for b in range(blocks):
        total = parts[0][b].astype(jnp.float32)
        for part in parts[1:]:
            total = total + part[b].astype(jnp.float32)
        scratch[...] = total
        for k in range(k_out):
            out_ref[k, :, b * tile : (b + 1) * tile] = scratch[pl.ds(k, levels, stride=k_out), :]


def finish(parts, k_out):
    blocks, rows, tile = parts[0].shape
    return pl.pallas_call(
        functools.partial(finish_kernel, k_out),
        out_shape=jax.ShapeDtypeStruct((k_out, rows // k_out, blocks * tile), jnp.float32),
        in_specs=[spec(VMEM)] * len(parts),
        out_specs=spec(VMEM),
        scratch_shapes=[VMEM((rows, tile), jnp.float32)],
        compiler_params=params(16),
    )(*parts)


def reduce_rows(slots, k_out, axis):
    n = slots.shape[0]
    parts = {p: [slots[p]] for p in range(n)}
    bit = 1
    while bit < n:
        for p in sorted((p for p in parts if p & bit), reverse=True):
            have = parts.pop(p)
            if len(have) > 1:
                value = functools.reduce(jnp.add, [x.astype(jnp.float32) for x in have])
                value = value.astype(BF16)
            else:
                value = have[0]
            moved = lax.ppermute(value, axis, [(i, i ^ bit) for i in range(n)])
            parts[p ^ bit].append(moved)
        bit *= 2
    return finish(parts[0], k_out)


def shards(tile_values, tile_row, tile_block, tile_count, tile_owner, cut_index, gradients):
    owners = lax.axis_size("feat")
    row_groups = lax.axis_size("rows")
    tile_dev, tile = tile_values.shape[:2]
    levels = cut_index.shape[0] + 1
    k_out, rows_dev = gradients.shape
    row_blocks = rows_dev // tile
    fb_dev = cut_index.shape[1] // tile
    per_tile = tile // ROWS_G
    capacity = max(2, 2 * tile_dev // owners) * per_tile
    unit = per_tile
    units = capacity // unit
    static = [max(1, units * i // 48) * unit for i in CHUNKS]
    while sum(static) >= capacity:
        static.pop()
    turn = min(TURN, capacity // per_tile // 12 + 1) * unit
    left = -(-(capacity - sum(static)) // turn) * turn
    me = lax.axis_index("feat").astype(jnp.int32)
    sent, skip = pack(
        me[None], tile_owner[:, 0], tile_count, tile_block, tile_row, gradients, tile_values,
        static + [left], unit, owners,
    )

    n = 2 * cut_index + (1 - 10 * (levels - 1))
    n = jnp.where(jnp.abs(n) > 256, n - 1, n)
    cuts = n.astype(jnp.float32) / 128.0
    cuts = jnp.concatenate([jnp.full((1, fb_dev * tile), -512.0, jnp.float32), cuts], axis=0)
    cuts = jnp.transpose(cuts.reshape(levels, fb_dev, tile), (1, 0, 2))

    def exchange(pieces):
        moved = [
            lax.ppermute(pieces[d], "feat", [(i, (i + d) % owners) for i in range(owners)])
            for d in range(1, owners)
        ]
        return [pieces[0]] + moved

    got = []
    for number in range(len(static)):
        pieces = sent[number]
        if number > 1:
            got[number - 2], pieces = lax.optimization_barrier((got[number - 2], pieces))
        got.append(exchange(pieces))

    heads = jnp.stack([x[:skip] for x in got[0]], axis=0)
    digits = heads[:, skip - 2 :].astype(jnp.int32)
    info = digits[:, 0] * DIGIT + digits[:, 1]
    grads = heads[:, : skip - 2].reshape(owners * row_blocks, k_out, tile)
    nothing = jnp.zeros_like(grads)
    grads = jnp.stack(
        [jnp.concatenate([grads, nothing], axis=1), jnp.concatenate([nothing, grads], axis=1)],
        axis=0,
    )
    mine = lax.axis_index("rows").astype(jnp.int32)

    most = jnp.max(info[:, 4, -1])
    turns = (most - sum(static) + turn - 1) // turn

    def which(low, fresh=0):
        return jnp.stack([jnp.asarray(x, jnp.int32) for x in (low, turns, mine, fresh)])

    def more(carry):
        return carry[0] < turns

    def step(carry):
        r, hist = carry
        pieces = [lax.dynamic_slice_in_dim(x, r * turn, turn, axis=0) for x in sent[-1]]
        hist = add_tiles(
            hist,
            which(sum(static) + r * turn, r == 0),
            info,
            exchange(pieces),
            grads,
            cuts,
            0,
            unit,
        )
        return r + 1, hist

    extra = unwritten((fb_dev, levels, k_out, tile))
    _, extra = lax.while_loop(more, step, (jnp.int32(0), extra))
    extra, grads = lax.optimization_barrier((extra, grads))
    hist, low = None, 0
    for number, size in enumerate(static):
        last = {"slots": row_groups, "more": extra} if number == len(static) - 1 else {}
        hist = add_tiles(
            hist, which(low), info, got[number], grads, cuts, 0 if number else skip, unit, **last
        )
        low += size
    return reduce_rows(hist, k_out, "rows")


def solution(mesh):
    placed = (
        P(("grp", "feat", "rows"), None, None),
        P(("grp", "feat", "rows")),
        P(("grp", "feat", "rows")),
        P(("grp", "feat", "rows")),
        P(("grp", "feat", "rows"), None),
        P(None, ("grp", "feat")),
        P(None, ("grp", "feat", "rows")),
    )
    return jax.shard_map(
        shards,
        mesh=mesh,
        in_specs=placed,
        out_specs=P(None, None, ("grp", "feat", "rows")),
        check_vma=False,
    )
```

```python
import functools

import jax
import jax.numpy as jnp
from jax import lax
from jax.experimental import pallas as pl
from jax.experimental.pallas import tpu as pltpu
from jax.sharding import PartitionSpec as P

ROWS_G = 8
PACKED = 16
VMEM = pltpu.VMEM
SMEM = pltpu.SMEM
ANY = pl.ANY
BF16 = jnp.bfloat16
INFO = 8
CHUNKS = (3, 7, 6, 5, 5, 5)
TURN = 4
AT_ONCE = 8
DIGIT = 256
PACK_MIB = 56


def params(mib):
    return pltpu.CompilerParams(vmem_limit_bytes=mib << 20)


def spec(space):
    return pl.BlockSpec(memory_space=space)


def cost(flops, mib):
    return pl.CostEstimate(flops=flops, bytes_accessed=mib << 20, transcendentals=0)


def log2(n):
    assert n & (n - 1) == 0
    return n.bit_length() - 1


def shifted(x, n):
    return lax.shift_right_logical(x, jnp.int32(log2(n)))


def wrapped(x, n):
    return jnp.where(x < 0, x + n, x)


def as_bf16(x):
    return x.astype(jnp.float32).astype(BF16)


def pack_kernel(
    sizes, unit, me_ref, owner_ref, count_ref, block_ref, row_ref, grads_hbm, values_hbm, *rest
):
    number = len(sizes)
    slots, lanes = rest[-4].shape[0], rest[-4].shape[2]
    outs = rest[: number * slots]
    scratch, values, heads, grads, info, lines, cursor, sem = rest[number * slots :]
    tiles, per_tile, _, tile = values.shape
    k_out, row_blocks = grads.shape[0], grads.shape[1] // tile
    parts = 4 if tiles % 4 == 0 else 1
    span = tiles // parts
    loads = [
        pltpu.make_async_copy(
            values_hbm.at[pl.ds(i * span, span)], values.at[pl.ds(i * span, span)], sem.at[i]
        )
        for i in range(parts)
    ] + [pltpu.make_async_copy(grads_hbm, grads, sem.at[parts])]
    for load in loads:
        load.start()
    me = me_ref[0]
    units = sum(sizes) // unit
    for d in range(slots):
        cursor[0, d] = 0
        cursor[1, d] = 0
        for u in range(units + 1):
            info[d, 4, u] = lanes
            info[d, 5, u] = lanes
    for i in range(parts):
        loads[i].wait()

        def place(t, carry):
            d = wrapped(owner_ref[t] - me, slots)
            at, n = cursor[0, d], cursor[1, d]
            count = count_ref[t]
            end = at + shifted(count + (ROWS_G * tile - 1), ROWS_G * tile)
            cursor[0, d] = end
            cursor[1, d] = n + 1
            scratch[d, pl.ds(at, per_tile)] = values[t]
            info[d, 0, n] = at
            info[d, 1, n] = count
            info[d, 2, n] = block_ref[t]
            info[d, 3, n] = row_ref[t]
            u = shifted(end - 1, unit)
            info[d, 4, jnp.where(u * unit >= at, u, lanes - 3)] = n
            u = shifted(end, unit)
            info[d, 5, jnp.where(u * unit > at, u, lanes - 3)] = n + 1
            return carry

        lax.fori_loop(i * span, (i + 1) * span, place, 0, unroll=4)
    most = cursor[0, 0]
    for d in range(1, slots):
        most = jnp.maximum(most, cursor[0, d])
    for d in range(slots):
        info[d, 4, lanes - 2] = cursor[1, d]
        info[d, 4, lanes - 1] = most
    listed = pltpu.make_async_copy(info, lines, sem.at[parts + 1])
    listed.start()
    loads[parts].wait()
    stack = [grads[:, b * tile : (b + 1) * tile] for b in range(row_blocks)]
    listed.wait()
    for d in range(slots):
        for b in range(row_blocks):
            heads[d, b] = stack[b]
        heads[d, row_blocks] = as_bf16(shifted(lines[d], DIGIT))
        heads[d, row_blocks + 1] = as_bf16(lines[d] & (DIGIT - 1))
    copies = []
    start, at = 0, parts + 2
    for c, size in enumerate(sizes):
        skip = heads.shape[1] if c == 0 else 0
        for d in range(slots):
            out = outs[c * slots + d]
            pairs = [(scratch.at[d, pl.ds(start, size)], out.at[pl.ds(skip, size)])]
            if skip:
                pairs += [(heads.at[d], out.at[pl.ds(0, skip)])]
            for source, target in pairs:
                copies.append(pltpu.make_async_copy(source, target, sem.at[at]))
                at += 1
        start += size
    always, rare = copies[:-slots], copies[-slots:]
    for copy in always:
        copy.start()

    @pl.when(most > start - sizes[-1])
    def _():
        for copy in rare:
            copy.start()
        for copy in rare:
            copy.wait()

    for copy in always:
        copy.wait()


def pack(me, owner, count, block, row, grads, values, sizes, unit, slots):
    tiles, tile = values.shape[0], values.shape[1]
    values = values.reshape(tiles, tile // ROWS_G, ROWS_G, tile)
    room = sum(sizes)
    lanes = 128
    assert max(2, 2 * tiles // slots) < lanes - 3 and room // unit < lanes - 3
    assert lanes == tile and INFO == ROWS_G == grads.shape[0]
    head = grads.size // (ROWS_G * tile) + 2
    shapes = [
        jax.ShapeDtypeStruct((size + (head if number == 0 else 0), ROWS_G, tile), BF16)
        for number, size in enumerate(sizes)
        for _ in range(slots)
    ]
    outs = pl.pallas_call(
        functools.partial(pack_kernel, sizes, unit),
        out_shape=shapes,
        in_specs=[spec(SMEM)] * 5 + [spec(ANY)] * 2,
        out_specs=[spec(ANY)] * len(shapes),
        scratch_shapes=[
            VMEM((slots, room, ROWS_G, tile), BF16),
            VMEM(values.shape, BF16),
            VMEM((slots, head, ROWS_G, tile), BF16),
            VMEM(grads.shape, BF16),
            SMEM((slots, INFO, lanes), jnp.int32),
            VMEM((slots, INFO, lanes), jnp.int32),
            SMEM((2, slots), jnp.int32),
            pltpu.SemaphoreType.DMA((6 + (len(sizes) + 1) * slots,)),
        ],
        compiler_params=params(PACK_MIB),
        cost_estimate=cost(0, 8),
    )(me, owner, count, block, row, grads, values)
    pieces = [list(outs[i * slots : (i + 1) * slots]) for i in range(len(sizes))]
    return pieces, head


def hist_kernel(kind, skip, senders, unit, row_blocks, which_ref, info_ref, *refs):
    first, last = kind
    got_refs, (grads_ref, cuts_ref), refs = (
        refs[:senders],
        refs[senders : senders + 2],
        refs[senders + 2 :],
    )
    if not first:
        before_ref, refs = refs[0], refs[1:]
    if last:
        more_ref, out_ref, hist_ref, got, list_ref, sem, extra = refs
    else:
        hist_ref, got, list_ref, sem = refs
    length, tile = got_refs[0].shape[0] - skip, got_refs[0].shape[2]
    per_tile = tile // ROWS_G
    blocks, levels = cuts_ref.shape[:2]
    k_out, lanes = hist_ref.shape[2], info_ref.shape[2]
    low = which_ref[0]
    copies = [
        pltpu.make_async_copy(
            got_refs[s].at[pl.ds(skip, length)],
            got.at[pl.ds(per_tile + s * length, length)],
            sem.at[s],
        )
        for s in range(senders)
    ]
    for copy in copies:
        copy.start()
    found = jnp.int32(0)
    for s in range(senders):
        tiles = info_ref[s, 4, lanes - 2]
        begin = jnp.minimum(info_ref[s, 4, shifted(low, unit)], tiles)
        end = jnp.minimum(info_ref[s, 5, shifted(low + length, unit)], tiles)

        def put(i, at, s=s):
            list_ref[at] = s * lanes + i
            return at + 1

        found = lax.fori_loop(begin, end, put, found)
    list_ref[found] = -1

    def clear(b, carry):
        hist_ref[b] = jnp.zeros(hist_ref.shape[1:], jnp.float32)
        return carry

    def keep(b, carry):
        hist_ref[b] = before_ref[b]
        return carry

    if first:
        lax.fori_loop(0, blocks, clear, 0)
    else:
        fresh = which_ref[3] > 0
        lax.fori_loop(0, jnp.where(fresh, blocks, 0), clear, 0)
        lax.fori_loop(0, jnp.where(fresh, 0, blocks), keep, 0)
    for copy in copies:
        copy.wait()
    row = as_bf16(lax.broadcasted_iota(jnp.int32, (tile, tile), 0))
    lane = as_bf16(lax.broadcasted_iota(jnp.int32, (tile, tile), 1))
    one, zero = jnp.ones((tile, tile), BF16), jnp.zeros((tile, tile), BF16)
    per = ROWS_G * tile

    def entry(p):
        e = list_ref[p]
        s, i, real = e >> log2(lanes), e & (lanes - 1), e >= 0
        at = jnp.where(real, info_ref[s & (senders - 1), 0, i], low)
        block = jnp.where(real, info_ref[s & (senders - 1), 2, i], 0)
        count = jnp.where(real, info_ref[s & (senders - 1), 1, i], 0)
        line = jnp.where(real, s * row_blocks + info_ref[s & (senders - 1), 3, i], 0)
        start = per_tile + jnp.where(real, s, 0) * length + at - low
        return start, block, jnp.minimum(count, (low + length - at) * per), (low - at) * ROWS_G, line

    def load(p):
        start, block, count, above, line = entry(p)
        values = got[pl.ds(start, per_tile)].reshape(tile, tile)
        whole = as_bf16(shifted(count, tile))
        part = as_bf16(count & (tile - 1))
        live = ((row < whole) | ((row == whole) & (lane < part))) & (row >= as_bf16(above))
        values = jnp.where(live, values, jnp.full_like(values, -1000.0))
        return block, values, line

    def pair(p):
        block_a, va, line_a = load(p)
        block_b, vb, line_b = load(p + 1)
        left = jnp.concatenate([grads_ref[0, line_a], grads_ref[1, line_b]], axis=1)
        for c in range(0, levels, 2):
            columns = []
            for d in (c, c + 1):
                cut_a = jnp.broadcast_to(cuts_ref[block_a, d : d + 1], (tile, tile))
                cut_b = jnp.broadcast_to(cuts_ref[block_b, d : d + 1], (tile, tile))
                columns.append(
                    jnp.concatenate(
                        [
                            jnp.where(va > cut_a.astype(BF16), one, zero),
                            jnp.where(vb > cut_b.astype(BF16), one, zero),
                        ],
                        axis=0,
                    )
                )
            sums = jnp.dot(
                left, jnp.concatenate(columns, axis=1), preferred_element_type=jnp.float32
            )
            hist_ref[block_a, c] += sums[:k_out, :tile]
            hist_ref[block_a, c + 1] += sums[:k_out, tile:]
            hist_ref[block_b, c] += sums[k_out:, :tile]
            hist_ref[block_b, c + 1] += sums[k_out:, tile:]

    def group(i, carry):
        for j in range(0, AT_ONCE, 2):
            pair(AT_ONCE * i + j)
        return carry

    whole_groups = found >> log2(AT_ONCE)
    lax.fori_loop(0, whole_groups, group, 0)

    def single(i, carry):
        pair(2 * i)
        return carry

    lax.fori_loop(whole_groups * (AT_ONCE // 2), (found + 1) >> 1, single, 0)
    if not last:
        return

    @pl.when(which_ref[1] > 0)
    def _():
        def add(b, carry):
            copy = pltpu.make_async_copy(more_ref.at[b], extra, sem.at[senders])
            copy.start()
            copy.wait()
            hist_ref[b] += extra[...]
            return carry

        lax.fori_loop(0, blocks, add, 0)

    slots, per_slot = out_ref.shape[0], out_ref.shape[1]
    me = which_ref[2]

    def step(i, carry):
        for slot in range(slots):
            above = hist_ref[(slot ^ me) * per_slot + i]
            below = jnp.concatenate(
                [above[1:], jnp.zeros((1, k_out, tile), jnp.float32)], axis=0
            )
            out_ref[slot, i] = (above - below).reshape(levels * k_out, tile).astype(BF16)
        return carry

    lax.fori_loop(0, per_slot, step, 0)


def add_tiles(hist, which, info, got, grads, cuts, skip, unit, slots=0, more=None):
    first, last = hist is None, slots > 0
    senders, length, tile = len(got), got[0].shape[0] - skip, got[0].shape[2]
    blocks, levels = cuts.shape[0], cuts.shape[1]
    k_out = grads.shape[2] // 2
    args = [which, info, *got, grads, cuts]
    specs = [spec(SMEM)] * 2 + [spec(ANY)] * senders + [spec(VMEM)] * 2
    whole = jax.ShapeDtypeStruct((blocks, levels, k_out, tile), jnp.float32)
    outs, aliases = [whole], {}
    if last:
        outs = [jax.ShapeDtypeStruct((slots, blocks // slots, levels * k_out, tile), BF16), whole]
    if not first:
        aliases = {len(args): len(outs) - 1}
        args.append(hist)
        specs.append(spec(VMEM))
    if last:
        args.append(more)
        specs.append(spec(ANY))
    result = pl.pallas_call(
        functools.partial(
            hist_kernel, (first, last), skip, senders, unit, grads.shape[1] // senders
        ),
        out_shape=outs,
        in_specs=specs,
        out_specs=[spec(VMEM)] * len(outs),
        scratch_shapes=[
            VMEM((senders * length + 2 * (tile // ROWS_G), ROWS_G, tile), BF16),
            SMEM((senders * (length + 1) + AT_ONCE,), jnp.int32),
            pltpu.SemaphoreType.DMA((senders + 1,)),
        ]
        + ([VMEM(whole.shape[1:], jnp.float32)] if last else []),
        input_output_aliases=aliases,
        compiler_params=params(28),
        cost_estimate=cost(10**10, 24),
    )(*args)
    return result[0]


def unwritten(shape):
    return pl.pallas_call(
        lambda out_ref: None,
        out_shape=jax.ShapeDtypeStruct(shape, jnp.float32),
        out_specs=spec(ANY),
        compiler_params=params(PACK_MIB),
    )()


def finish_kernel(k_out, *refs):
    parts, out_ref, scratch = refs[:-2], refs[-2], refs[-1]
    blocks, rows, tile = parts[0].shape
    levels = rows // k_out
    for b in range(blocks):
        total = parts[0][b].astype(jnp.float32)
        for part in parts[1:]:
            total = total + part[b].astype(jnp.float32)
        scratch[...] = total
        for k in range(k_out):
            out_ref[k, :, b * tile : (b + 1) * tile] = scratch[pl.ds(k, levels, stride=k_out), :]


def finish(parts, k_out):
    blocks, rows, tile = parts[0].shape
    return pl.pallas_call(
        functools.partial(finish_kernel, k_out),
        out_shape=jax.ShapeDtypeStruct((k_out, rows // k_out, blocks * tile), jnp.float32),
        in_specs=[spec(VMEM)] * len(parts),
        out_specs=spec(VMEM),
        scratch_shapes=[VMEM((rows, tile), jnp.float32)],
        compiler_params=params(16),
    )(*parts)


def reduce_rows(slots, k_out, axis):
    n = slots.shape[0]
    parts = {p: [slots[p]] for p in range(n)}
    bit = 1
    while bit < n:
        for p in sorted((p for p in parts if p & bit), reverse=True):
            have = parts.pop(p)
            if len(have) > 1:
                value = functools.reduce(jnp.add, [x.astype(jnp.float32) for x in have])
                value = value.astype(BF16)
            else:
                value = have[0]
            moved = lax.ppermute(value, axis, [(i, i ^ bit) for i in range(n)])
            parts[p ^ bit].append(moved)
        bit *= 2
    return finish(parts[0], k_out)


def shards(tile_values, tile_row, tile_block, tile_count, tile_owner, cut_index, gradients):
    owners = lax.axis_size("feat")
    row_groups = lax.axis_size("rows")
    tile_dev, tile = tile_values.shape[:2]
    levels = cut_index.shape[0] + 1
    k_out, rows_dev = gradients.shape
    row_blocks = rows_dev // tile
    fb_dev = cut_index.shape[1] // tile
    per_tile = tile // ROWS_G
    capacity = max(2, 2 * tile_dev // owners) * per_tile
    unit = per_tile
    units = capacity // unit
    static = [max(1, units * i // 48) * unit for i in CHUNKS]
    while sum(static) >= capacity:
        static.pop()
    turn = min(TURN, capacity // per_tile // 12 + 1) * unit
    left = -(-(capacity - sum(static)) // turn) * turn
    me = lax.axis_index("feat").astype(jnp.int32)
    sent, skip = pack(
        me[None], tile_owner[:, 0], tile_count, tile_block, tile_row, gradients, tile_values,
        static + [left], unit, owners,
    )

    n = 2 * cut_index + (1 - 10 * (levels - 1))
    n = jnp.where(jnp.abs(n) > 256, n - 1, n)
    cuts = n.astype(jnp.float32) / 128.0
    cuts = jnp.concatenate([jnp.full((1, fb_dev * tile), -512.0, jnp.float32), cuts], axis=0)
    cuts = jnp.transpose(cuts.reshape(levels, fb_dev, tile), (1, 0, 2))

    def exchange(pieces):
        moved = [
            lax.ppermute(pieces[d], "feat", [(i, (i + d) % owners) for i in range(owners)])
            for d in range(1, owners)
        ]
        return [pieces[0]] + moved

    got = []
    for number in range(len(static)):
        pieces = sent[number]
        if number > 1:
            _, pieces = lax.optimization_barrier((got[number - 2], pieces))
        got.append(exchange(pieces))

    heads = jnp.stack([x[:skip] for x in got[0]], axis=0)
    digits = heads[:, skip - 2 :].astype(jnp.int32)
    info = digits[:, 0] * DIGIT + digits[:, 1]
    grads = heads[:, : skip - 2].reshape(owners * row_blocks, k_out, tile)
    nothing = jnp.zeros_like(grads)
    grads = jnp.stack(
        [jnp.concatenate([grads, nothing], axis=1), jnp.concatenate([nothing, grads], axis=1)],
        axis=0,
    )
    mine = lax.axis_index("rows").astype(jnp.int32)

    most = jnp.max(info[:, 4, -1])
    turns = (most - sum(static) + turn - 1) // turn

    def which(low, fresh=0):
        return jnp.stack([jnp.asarray(x, jnp.int32) for x in (low, turns, mine, fresh)])

    def more(carry):
        return carry[0] < turns

    def step(carry):
        r, hist = carry
        pieces = [lax.dynamic_slice_in_dim(x, r * turn, turn, axis=0) for x in sent[-1]]
        hist = add_tiles(
            hist,
            which(sum(static) + r * turn, r == 0),
            info,
            exchange(pieces),
            grads,
            cuts,
            0,
            unit,
        )
        return r + 1, hist

    extra = unwritten((fb_dev, levels, k_out, tile))
    _, extra = lax.while_loop(more, step, (jnp.int32(0), extra))
    extra, grads = lax.optimization_barrier((extra, grads))
    hist, low = None, 0
    for number, size in enumerate(static):
        last = {"slots": row_groups, "more": extra} if number == len(static) - 1 else {}
        hist = add_tiles(
            hist, which(low), info, got[number], grads, cuts, 0 if number else skip, unit, **last
        )
        low += size
    return reduce_rows(hist, k_out, "rows")


def solution(mesh):
    placed = (
        P(("grp", "feat", "rows"), None, None),
        P(("grp", "feat", "rows")),
        P(("grp", "feat", "rows")),
        P(("grp", "feat", "rows")),
        P(("grp", "feat", "rows"), None),
        P(None, ("grp", "feat")),
        P(None, ("grp", "feat", "rows")),
    )
    return jax.shard_map(
        shards,
        mesh=mesh,
        in_specs=placed,
        out_specs=P(None, None, ("grp", "feat", "rows")),
        check_vma=False,
    )
```

```python
import functools

import jax
import jax.numpy as jnp
from jax import lax
from jax.experimental import pallas as pl
from jax.experimental.pallas import tpu as pltpu
from jax.sharding import PartitionSpec as P

ROWS_G = 8
PACKED = 16
VMEM = pltpu.VMEM
SMEM = pltpu.SMEM
ANY = pl.ANY
BF16 = jnp.bfloat16
INFO = 8
CHUNKS = (3, 7, 6, 5, 5, 5)
TURN = 4
AT_ONCE = 8
DIGIT = 256
PACK_MIB = 56


def params(mib):
    return pltpu.CompilerParams(vmem_limit_bytes=mib << 20)


def spec(space):
    return pl.BlockSpec(memory_space=space)


def cost(flops, mib):
    return pl.CostEstimate(flops=flops, bytes_accessed=mib << 20, transcendentals=0)


def log2(n):
    assert n & (n - 1) == 0
    return n.bit_length() - 1


def shifted(x, n):
    return lax.shift_right_logical(x, jnp.int32(log2(n)))


def wrapped(x, n):
    return jnp.where(x < 0, x + n, x)


def as_bf16(x):
    return x.astype(jnp.float32).astype(BF16)


def pack_kernel(
    sizes, unit, me_ref, owner_ref, count_ref, block_ref, row_ref, grads_hbm, values_hbm, *rest
):
    number = len(sizes)
    slots, lanes = rest[-4].shape[0], rest[-4].shape[2]
    outs = rest[: number * slots]
    scratch, values, heads, grads, info, lines, cursor, sem = rest[number * slots :]
    tiles, per_tile, _, tile = values.shape
    k_out, row_blocks = grads.shape[0], grads.shape[1] // tile
    parts = 4 if tiles % 4 == 0 else 1
    span = tiles // parts
    loads = [
        pltpu.make_async_copy(
            values_hbm.at[pl.ds(i * span, span)], values.at[pl.ds(i * span, span)], sem.at[i]
        )
        for i in range(parts)
    ] + [pltpu.make_async_copy(grads_hbm, grads, sem.at[parts])]
    for load in loads:
        load.start()
    me = me_ref[0]
    units = sum(sizes) // unit
    for d in range(slots):
        cursor[0, d] = 0
        cursor[1, d] = 0
        for u in range(units + 1):
            info[d, 4, u] = lanes
            info[d, 5, u] = lanes
    for i in range(parts):
        loads[i].wait()

        def place(t, carry):
            d = wrapped(owner_ref[t] - me, slots)
            at, n = cursor[0, d], cursor[1, d]
            count = count_ref[t]
            end = at + shifted(count + (ROWS_G * tile - 1), ROWS_G * tile)
            cursor[0, d] = end
            cursor[1, d] = n + 1
            scratch[d, pl.ds(at, per_tile)] = values[t]
            info[d, 0, n] = at
            info[d, 1, n] = count
            info[d, 2, n] = block_ref[t]
            info[d, 3, n] = row_ref[t]
            u = shifted(end - 1, unit)
            info[d, 4, jnp.where(u * unit >= at, u, lanes - 3)] = n
            u = shifted(end, unit)
            info[d, 5, jnp.where(u * unit > at, u, lanes - 3)] = n + 1
            return carry

        lax.fori_loop(i * span, (i + 1) * span, place, 0, unroll=4)
    most = cursor[0, 0]
    for d in range(1, slots):
        most = jnp.maximum(most, cursor[0, d])
    for d in range(slots):
        info[d, 4, lanes - 2] = cursor[1, d]
        info[d, 4, lanes - 1] = most
    listed = pltpu.make_async_copy(info, lines, sem.at[parts + 1])
    listed.start()
    loads[parts].wait()
    stack = [grads[:, b * tile : (b + 1) * tile] for b in range(row_blocks)]
    listed.wait()
    for d in range(slots):
        for b in range(row_blocks):
            heads[d, b] = stack[b]
        heads[d, row_blocks] = as_bf16(shifted(lines[d], DIGIT))
        heads[d, row_blocks + 1] = as_bf16(lines[d] & (DIGIT - 1))
    copies = []
    start, at = 0, parts + 2
    for c, size in enumerate(sizes):
        skip = heads.shape[1] if c == 0 else 0
        for d in range(slots):
            out = outs[c * slots + d]
            pairs = [(scratch.at[d, pl.ds(start, size)], out.at[pl.ds(skip, size)])]
            if skip:
                pairs += [(heads.at[d], out.at[pl.ds(0, skip)])]
            for source, target in pairs:
                copies.append(pltpu.make_async_copy(source, target, sem.at[at]))
                at += 1
        start += size
    always, rare = copies[:-slots], copies[-slots:]
    for copy in always:
        copy.start()

    @pl.when(most > start - sizes[-1])
    def _():
        for copy in rare:
            copy.start()
        for copy in rare:
            copy.wait()

    for copy in always:
        copy.wait()


def pack(me, owner, count, block, row, grads, values, sizes, unit, slots):
    tiles, tile = values.shape[0], values.shape[1]
    values = values.reshape(tiles, tile // ROWS_G, ROWS_G, tile)
    room = sum(sizes)
    lanes = 128
    assert max(2, 2 * tiles // slots) < lanes - 3 and room // unit < lanes - 3
    assert lanes == tile and INFO == ROWS_G == grads.shape[0]
    head = grads.size // (ROWS_G * tile) + 2
    shapes = [
        jax.ShapeDtypeStruct((size + (head if number == 0 else 0), ROWS_G, tile), BF16)
        for number, size in enumerate(sizes)
        for _ in range(slots)
    ]
    outs = pl.pallas_call(
        functools.partial(pack_kernel, sizes, unit),
        out_shape=shapes,
        in_specs=[spec(SMEM)] * 5 + [spec(ANY)] * 2,
        out_specs=[spec(ANY)] * len(shapes),
        scratch_shapes=[
            VMEM((slots, room, ROWS_G, tile), BF16),
            VMEM(values.shape, BF16),
            VMEM((slots, head, ROWS_G, tile), BF16),
            VMEM(grads.shape, BF16),
            SMEM((slots, INFO, lanes), jnp.int32),
            VMEM((slots, INFO, lanes), jnp.int32),
            SMEM((2, slots), jnp.int32),
            pltpu.SemaphoreType.DMA((6 + (len(sizes) + 1) * slots,)),
        ],
        compiler_params=params(PACK_MIB),
        cost_estimate=cost(0, 8),
    )(me, owner, count, block, row, grads, values)
    pieces = [list(outs[i * slots : (i + 1) * slots]) for i in range(len(sizes))]
    return pieces, head


def hist_kernel(kind, skip, senders, unit, row_blocks, which_ref, info_ref, *refs):
    first, last = kind
    got_refs, (grads_ref, cuts_ref), refs = (
        refs[:senders],
        refs[senders : senders + 2],
        refs[senders + 2 :],
    )
    if not first:
        before_ref, refs = refs[0], refs[1:]
    if last:
        more_ref, out_ref, hist_ref, got, list_ref, sem, extra = refs
    else:
        hist_ref, got, list_ref, sem = refs
    length, tile = got_refs[0].shape[0] - skip, got_refs[0].shape[2]
    per_tile = tile // ROWS_G
    blocks, levels = cuts_ref.shape[:2]
    k_out, lanes = hist_ref.shape[2], info_ref.shape[2]
    low = which_ref[0]
    copies = [
        pltpu.make_async_copy(
            got_refs[s].at[pl.ds(skip, length)],
            got.at[pl.ds(per_tile + s * length, length)],
            sem.at[s],
        )
        for s in range(senders)
    ]
    for copy in copies:
        copy.start()
    found = jnp.int32(0)
    for s in range(senders):
        tiles = info_ref[s, 4, lanes - 2]
        begin = jnp.minimum(info_ref[s, 4, shifted(low, unit)], tiles)
        end = jnp.minimum(info_ref[s, 5, shifted(low + length, unit)], tiles)

        def put(i, at, s=s):
            list_ref[at] = s * lanes + i
            return at + 1

        found = lax.fori_loop(begin, end, put, found)
    list_ref[found] = -1

    def clear(b, carry):
        hist_ref[b] = jnp.zeros(hist_ref.shape[1:], jnp.float32)
        return carry

    def keep(b, carry):
        hist_ref[b] = before_ref[b]
        return carry

    if first:
        lax.fori_loop(0, blocks, clear, 0)
    else:
        fresh = which_ref[3] > 0

        @pl.when(fresh)
        def _():
            lax.fori_loop(0, blocks, clear, 0)

        @pl.when(jnp.logical_not(fresh))
        def _():
            lax.fori_loop(0, blocks, keep, 0, unroll=4)
    for copy in copies:
        copy.wait()
    row = as_bf16(lax.broadcasted_iota(jnp.int32, (tile, tile), 0))
    lane = as_bf16(lax.broadcasted_iota(jnp.int32, (tile, tile), 1))
    one, zero = jnp.ones((tile, tile), BF16), jnp.zeros((tile, tile), BF16)
    per = ROWS_G * tile

    def entry(p):
        e = list_ref[p]
        s, i, real = e >> log2(lanes), e & (lanes - 1), e >= 0
        at = jnp.where(real, info_ref[s & (senders - 1), 0, i], low)
        block = jnp.where(real, info_ref[s & (senders - 1), 2, i], 0)
        count = jnp.where(real, info_ref[s & (senders - 1), 1, i], 0)
        line = jnp.where(real, s * row_blocks + info_ref[s & (senders - 1), 3, i], 0)
        start = per_tile + jnp.where(real, s, 0) * length + at - low
        return start, block, jnp.minimum(count, (low + length - at) * per), (low - at) * ROWS_G, line

    def load(p):
        start, block, count, above, line = entry(p)
        values = got[pl.ds(start, per_tile)].reshape(tile, tile)
        whole = as_bf16(shifted(count, tile))
        part = as_bf16(count & (tile - 1))
        live = ((row < whole) | ((row == whole) & (lane < part))) & (row >= as_bf16(above))
        values = jnp.where(live, values, jnp.full_like(values, -1000.0))
        return block, values, line

    def pair(p):
        block_a, va, line_a = load(p)
        block_b, vb, line_b = load(p + 1)
        left = jnp.concatenate([grads_ref[0, line_a], grads_ref[1, line_b]], axis=1)
        for c in range(0, levels, 2):
            columns = []
            for d in (c, c + 1):
                cut_a = jnp.broadcast_to(cuts_ref[block_a, d : d + 1], (tile, tile))
                cut_b = jnp.broadcast_to(cuts_ref[block_b, d : d + 1], (tile, tile))
                columns.append(
                    jnp.concatenate(
                        [
                            jnp.where(va > cut_a.astype(BF16), one, zero),
                            jnp.where(vb > cut_b.astype(BF16), one, zero),
                        ],
                        axis=0,
                    )
                )
            sums = jnp.dot(
                left, jnp.concatenate(columns, axis=1), preferred_element_type=jnp.float32
            )
            hist_ref[block_a, c] += sums[:k_out, :tile]
            hist_ref[block_a, c + 1] += sums[:k_out, tile:]
            hist_ref[block_b, c] += sums[k_out:, :tile]
            hist_ref[block_b, c + 1] += sums[k_out:, tile:]

    def group(i, carry):
        for j in range(0, AT_ONCE, 2):
            pair(AT_ONCE * i + j)
        return carry

    whole_groups = found >> log2(AT_ONCE)
    lax.fori_loop(0, whole_groups, group, 0)

    def single(i, carry):
        pair(2 * i)
        return carry

    lax.fori_loop(whole_groups * (AT_ONCE // 2), (found + 1) >> 1, single, 0)
    if not last:
        return

    @pl.when(which_ref[1] > 0)
    def _():
        def add(b, carry):
            copy = pltpu.make_async_copy(more_ref.at[b], extra, sem.at[senders])
            copy.start()
            copy.wait()
            hist_ref[b] += extra[...]
            return carry

        lax.fori_loop(0, blocks, add, 0)

    slots, per_slot = out_ref.shape[0], out_ref.shape[1]
    me = which_ref[2]

    def step(i, carry):
        for slot in range(slots):
            above = hist_ref[(slot ^ me) * per_slot + i]
            below = jnp.concatenate(
                [above[1:], jnp.zeros((1, k_out, tile), jnp.float32)], axis=0
            )
            out_ref[slot, i] = (above - below).reshape(levels * k_out, tile).astype(BF16)
        return carry

    lax.fori_loop(0, per_slot, step, 0)


def add_tiles(hist, which, info, got, grads, cuts, skip, unit, slots=0, more=None):
    first, last = hist is None, slots > 0
    senders, length, tile = len(got), got[0].shape[0] - skip, got[0].shape[2]
    blocks, levels = cuts.shape[0], cuts.shape[1]
    k_out = grads.shape[2] // 2
    args = [which, info, *got, grads, cuts]
    specs = [spec(SMEM)] * 2 + [spec(ANY)] * senders + [spec(VMEM)] * 2
    whole = jax.ShapeDtypeStruct((blocks, levels, k_out, tile), jnp.float32)
    outs, aliases = [whole], {}
    if last:
        outs = [jax.ShapeDtypeStruct((slots, blocks // slots, levels * k_out, tile), BF16), whole]
    if not first:
        aliases = {len(args): len(outs) - 1}
        args.append(hist)
        specs.append(spec(VMEM))
    if last:
        args.append(more)
        specs.append(spec(ANY))
    result = pl.pallas_call(
        functools.partial(
            hist_kernel, (first, last), skip, senders, unit, grads.shape[1] // senders
        ),
        out_shape=outs,
        in_specs=specs,
        out_specs=[spec(VMEM)] * len(outs),
        scratch_shapes=[
            VMEM((senders * length + 2 * (tile // ROWS_G), ROWS_G, tile), BF16),
            SMEM((senders * (length + 1) + AT_ONCE,), jnp.int32),
            pltpu.SemaphoreType.DMA((senders + 1,)),
        ]
        + ([VMEM(whole.shape[1:], jnp.float32)] if last else []),
        input_output_aliases=aliases,
        compiler_params=params(28),
        cost_estimate=cost(10**10, 24),
    )(*args)
    return result[0]


def unwritten(shape):
    return pl.pallas_call(
        lambda out_ref: None,
        out_shape=jax.ShapeDtypeStruct(shape, jnp.float32),
        out_specs=spec(ANY),
        compiler_params=params(PACK_MIB),
    )()


def finish_kernel(k_out, *refs):
    parts, out_ref, scratch = refs[:-2], refs[-2], refs[-1]
    blocks, rows, tile = parts[0].shape
    levels = rows // k_out
    for b in range(blocks):
        total = parts[0][b].astype(jnp.float32)
        for part in parts[1:]:
            total = total + part[b].astype(jnp.float32)
        scratch[...] = total
        for k in range(k_out):
            out_ref[k, :, b * tile : (b + 1) * tile] = scratch[pl.ds(k, levels, stride=k_out), :]


def finish(parts, k_out):
    blocks, rows, tile = parts[0].shape
    return pl.pallas_call(
        functools.partial(finish_kernel, k_out),
        out_shape=jax.ShapeDtypeStruct((k_out, rows // k_out, blocks * tile), jnp.float32),
        in_specs=[spec(VMEM)] * len(parts),
        out_specs=spec(VMEM),
        scratch_shapes=[VMEM((rows, tile), jnp.float32)],
        compiler_params=params(16),
    )(*parts)


def reduce_rows(slots, k_out, axis):
    n = slots.shape[0]
    parts = {p: [slots[p]] for p in range(n)}
    bit = 1
    while bit < n:
        for p in sorted((p for p in parts if p & bit), reverse=True):
            have = parts.pop(p)
            if len(have) > 1:
                value = functools.reduce(jnp.add, [x.astype(jnp.float32) for x in have])
                value = value.astype(BF16)
            else:
                value = have[0]
            moved = lax.ppermute(value, axis, [(i, i ^ bit) for i in range(n)])
            parts[p ^ bit].append(moved)
        bit *= 2
    return finish(parts[0], k_out)


def shards(tile_values, tile_row, tile_block, tile_count, tile_owner, cut_index, gradients):
    owners = lax.axis_size("feat")
    row_groups = lax.axis_size("rows")
    tile_dev, tile = tile_values.shape[:2]
    levels = cut_index.shape[0] + 1
    k_out, rows_dev = gradients.shape
    row_blocks = rows_dev // tile
    fb_dev = cut_index.shape[1] // tile
    per_tile = tile // ROWS_G
    capacity = max(2, 2 * tile_dev // owners) * per_tile
    unit = per_tile
    units = capacity // unit
    static = [max(1, units * i // 48) * unit for i in CHUNKS]
    while sum(static) >= capacity:
        static.pop()
    turn = min(TURN, capacity // per_tile // 12 + 1) * unit
    left = -(-(capacity - sum(static)) // turn) * turn
    me = lax.axis_index("feat").astype(jnp.int32)
    sent, skip = pack(
        me[None], tile_owner[:, 0], tile_count, tile_block, tile_row, gradients, tile_values,
        static + [left], unit, owners,
    )

    n = 2 * cut_index + (1 - 10 * (levels - 1))
    n = jnp.where(jnp.abs(n) > 256, n - 1, n)
    cuts = n.astype(jnp.float32) / 128.0
    cuts = jnp.concatenate([jnp.full((1, fb_dev * tile), -512.0, jnp.float32), cuts], axis=0)
    cuts = jnp.transpose(cuts.reshape(levels, fb_dev, tile), (1, 0, 2))

    def exchange(pieces):
        moved = [
            lax.ppermute(pieces[d], "feat", [(i, (i + d) % owners) for i in range(owners)])
            for d in range(1, owners)
        ]
        return [pieces[0]] + moved

    got = []
    for number in range(len(static)):
        pieces = sent[number]
        if number > 1:
            _, pieces = lax.optimization_barrier((got[number - 2], pieces))
        got.append(exchange(pieces))

    heads = jnp.stack([x[:skip] for x in got[0]], axis=0)
    digits = heads[:, skip - 2 :].astype(jnp.int32)
    info = digits[:, 0] * DIGIT + digits[:, 1]
    grads = heads[:, : skip - 2].reshape(owners * row_blocks, k_out, tile)
    nothing = jnp.zeros_like(grads)
    grads = jnp.stack(
        [jnp.concatenate([grads, nothing], axis=1), jnp.concatenate([nothing, grads], axis=1)],
        axis=0,
    )
    mine = lax.axis_index("rows").astype(jnp.int32)

    most = jnp.max(info[:, 4, -1])
    turns = (most - sum(static) + turn - 1) // turn

    def which(low, fresh=0):
        return jnp.stack([jnp.asarray(x, jnp.int32) for x in (low, turns, mine, fresh)])

    def more(carry):
        return carry[0] < turns

    def step(carry):
        r, hist = carry
        pieces = [lax.dynamic_slice_in_dim(x, r * turn, turn, axis=0) for x in sent[-1]]
        hist = add_tiles(
            hist,
            which(sum(static) + r * turn, r == 0),
            info,
            exchange(pieces),
            grads,
            cuts,
            0,
            unit,
        )
        return r + 1, hist

    extra = unwritten((fb_dev, levels, k_out, tile))
    _, extra = lax.while_loop(more, step, (jnp.int32(0), extra))
    extra, grads = lax.optimization_barrier((extra, grads))
    hist, low = None, 0
    for number, size in enumerate(static):
        last = {"slots": row_groups, "more": extra} if number == len(static) - 1 else {}
        hist = add_tiles(
            hist, which(low), info, got[number], grads, cuts, 0 if number else skip, unit, **last
        )
        low += size
    return reduce_rows(hist, k_out, "rows")


def solution(mesh):
    placed = (
        P(("grp", "feat", "rows"), None, None),
        P(("grp", "feat", "rows")),
        P(("grp", "feat", "rows")),
        P(("grp", "feat", "rows")),
        P(("grp", "feat", "rows"), None),
        P(None, ("grp", "feat")),
        P(None, ("grp", "feat", "rows")),
    )
    return jax.shard_map(
        shards,
        mesh=mesh,
        in_specs=placed,
        out_specs=P(None, None, ("grp", "feat", "rows")),
        check_vma=False,
    )
```
